128 devices in a mesh: gx: 8 (over y, z_hi), gy: 16 (over x, z_lo, core).
Axes of the slice: x: 4, y: 4, z: 4 (z_hi: 2, z_lo: 2; z = z_hi * 2 + z_lo), core: 2. Of those that a mesh axis runs over, the one named last changes fastest.
Arguments:
- electric: float32 [3, 128, 128, 256], P(None, 'gx', 'gy'), may hold values from -1.5 to 1.5
- magnetic: float32 [3, 128, 128, 256], P(None, 'gx', 'gy'), may hold values from -6 to 6
- material: int32 [128, 128, 256], P('gx', 'gy'), may hold values from 0 to 7
- permittivity: float32 [8], replicated, may hold values from 1 to 4
- conductivity: float32 [8], replicated, may hold values from 0.01 to 1
Outputs:
- advanced_electric: float32 [3, 128, 128, 256], P(None, 'gx', 'gy')
- advanced_magnetic: float32 [3, 128, 128, 256], P(None, 'gx', 'gy')
The draws below stay inside these ranges and needn't reach their ends.
All inputs are finite; a program needn't handle non-finite values.
Results may differ from the reference program's by a relative error of at most 0.0003.
Values sent between devices are 32-bit elements; how exact they have to be, the bound alone decides.
No kernel may reach another device: no remote copies, remote signals or barrier semaphores. Data moves between devices by JAX's collectives and lax.ppermute only.
A program may use at most 64 MiB of HBM per device.

```python
import math
import jax
import jax.numpy as jnp
from jax import lax

CZ = 256
NMAT = 8
NX = 128
NY = 128


def plant(values, own_key, low, top_value):
    longest = values.shape.index(max(values.shape))
    spots = []
    for shift in (0, 1):
        where = [jax.random.randint(jax.random.fold_in(own_key, axis), (), 0, length) for axis, length in enumerate(values.shape)]
        where[longest] = (where[longest] + shift) % values.shape[longest]
        spots.append(tuple(where))
    return values.at[spots[0]].set(low).at[spots[1]].set(top_value)


def block_scale(stream_key, shape, shards, low, top_value):
    gain, own = 1.0, jax.random.fold_in(stream_key, 6)
    for axis_at, shards_of in shards:
        heights = jnp.exp(jax.random.uniform(jax.random.fold_in(own, axis_at), (shards_of,), jnp.float32, low / len(shards), top_value / len(shards)))
        gain = gain * jnp.repeat(heights, shape[axis_at] // shards_of).reshape([-1 if axis == axis_at else 1 for axis in range(len(shape))])
    return gain


def normal_values(own_key, dims, width, most, shards=(), held_as=jnp.bfloat16):
    factor_of = block_scale(own_key, dims, shards, -0.22, 0.18) if shards else 1.0
    array = jax.random.normal(own_key, dims, jnp.float32) * width * factor_of
    return jnp.minimum(jnp.maximum(array, -most), most).astype(held_as)


def setup_inputs(seed: int = 0) -> dict:
    key_list = jax.random.split(jax.random.key(seed), 6)
    return {
        "electric": normal_values(key_list[0], (3, NX, NY, CZ), 0.25, 1.5, ((1, 8), (2, 16)), jnp.float32),
        "magnetic": normal_values(key_list[1], (3, NX, NY, CZ), 1.0, 6.0, ((1, 8), (2, 16)), jnp.float32),
        "material": plant(jax.random.randint(key_list[2], (NX, NY, CZ), 0, NMAT), jax.random.fold_in(key_list[2], 1), 0, NMAT - 1).astype(jnp.int32),
        "permittivity": jnp.clip(jnp.exp(jax.random.uniform(key_list[3], (NMAT,), jnp.float32, math.log(1.0), math.log(4.0))), 1.0, 4.0),
        "conductivity": jnp.clip(jnp.exp(jax.random.uniform(key_list[4], (NMAT,), jnp.float32, math.log(0.01), math.log(1.0))), 0.01, 1.0),
    }


half_step = 12.0


def forward_diff(field, line_axis):
    length = field.shape[line_axis]
    zero_plane = jnp.zeros_like(lax.slice_in_dim(field, 0, 1, axis=line_axis))
    shifted = jnp.concatenate([lax.slice_in_dim(field, 1, length, axis=line_axis), zero_plane], axis=line_axis)
    return shifted - field


def backward_diff(field, line_axis):
    length = field.shape[line_axis]
    zero_plane = jnp.zeros_like(lax.slice_in_dim(field, 0, 1, axis=line_axis))
    shifted = jnp.concatenate([zero_plane, lax.slice_in_dim(field, 0, length - 1, axis=line_axis)], axis=line_axis)
    return field - shifted


def build_system(source, stiffness, position, line_length):
    below = jnp.where(position == 0, 0.0, -stiffness)
    above = jnp.where(position == line_length - 1, 0.0, -stiffness)
    diagonal = jnp.where(position == 0, 1.0 + stiffness, 1.0 + 2.0 * stiffness)
    return jnp.stack([below, diagonal, above, source])


def reduce_level(system, preceding, following):
    divisor_below = jnp.where(preceding[1] == 0.0, 1.0, preceding[1])
    divisor_above = jnp.where(following[1] == 0.0, 1.0, following[1])
    factor_below = -system[0] / divisor_below
    factor_above = -system[2] / divisor_above
    return jnp.stack([
        factor_below * preceding[0],
        system[1] + factor_below * preceding[2] + factor_above * following[0],
        factor_above * following[2],
        system[3] + factor_below * preceding[3] + factor_above * following[3],
    ])


def shift_local(system, stride, stack_axis, from_before):
    length = system.shape[stack_axis]
    zero_block = jnp.zeros_like(lax.slice_in_dim(system, 0, stride, axis=stack_axis))
    if from_before:
        return jnp.concatenate([zero_block, lax.slice_in_dim(system, 0, length - stride, axis=stack_axis)], axis=stack_axis)
    return jnp.concatenate([lax.slice_in_dim(system, stride, length, axis=stack_axis), zero_block], axis=stack_axis)


def solve_local(source, stiffness, line_axis):
    length = source.shape[line_axis]
    position = lax.broadcasted_iota(jnp.int32, source.shape, line_axis)
    system = build_system(source, stiffness, position, length)
    stride = 1
    while stride < length:
        system = reduce_level(system, shift_local(system, stride, line_axis + 1, True),
                              shift_local(system, stride, line_axis + 1, False))
        stride = stride * 2
    return system[3] / system[1]


def coefficients(permittivity, conductivity):
    denom_table = permittivity / half_step + 0.5 * conductivity
    damp_table = (permittivity / half_step - 0.5 * conductivity) / denom_table
    couple_table = 1.0 / denom_table
    return damp_table, couple_table


def reference(electric, magnetic, material, permittivity, conductivity):
    damp_table, couple_table = coefficients(permittivity, conductivity)
    damping = damp_table[material]
    coupling = couple_table[material]
    stiffness = half_step * coupling
    interim_z = magnetic[2] - half_step * forward_diff(electric[1], 0)
    interim_x = magnetic[0] - half_step * forward_diff(electric[2], 1)
    interim_y = magnetic[1] - half_step * forward_diff(electric[0], 2)
    center_x = solve_local(damping * electric[0] + coupling * (backward_diff(interim_z, 1) - backward_diff(magnetic[1], 2)), stiffness, 1)
    center_y = solve_local(damping * electric[1] + coupling * (backward_diff(interim_x, 2) - backward_diff(magnetic[2], 0)), stiffness, 2)
    center_z = solve_local(damping * electric[2] + coupling * (backward_diff(interim_y, 0) - backward_diff(magnetic[0], 1)), stiffness, 0)
    curl_for_z = half_step * forward_diff(center_x, 1)
    curl_for_x = half_step * forward_diff(center_y, 2)
    curl_for_y = half_step * forward_diff(center_z, 0)
    middle_z = interim_z + curl_for_z
    middle_x = interim_x + curl_for_x
    middle_y = interim_y + curl_for_y
    second_z = middle_z + curl_for_z
    second_x = middle_x + curl_for_x
    second_y = middle_y + curl_for_y
    final_x = solve_local(damping * center_x + coupling * (backward_diff(middle_z, 1) - backward_diff(second_y, 2)), stiffness, 2)
    final_y = solve_local(damping * center_y + coupling * (backward_diff(middle_x, 2) - backward_diff(second_z, 0)), stiffness, 0)
    final_z = solve_local(damping * center_z + coupling * (backward_diff(middle_y, 0) - backward_diff(second_x, 1)), stiffness, 1)
    magnet_z = second_z - half_step * forward_diff(final_y, 0)
    magnet_x = second_x - half_step * forward_diff(final_z, 1)
    magnet_y = second_y - half_step * forward_diff(final_x, 2)
    return jnp.stack([final_x, final_y, final_z]), jnp.stack([magnet_x, magnet_y, magnet_z])
```

```python
import jax
import jax.numpy as jnp
from jax import lax
from jax.experimental import pallas as pl
from jax.experimental.pallas import tpu as pltpu
from jax.sharding import PartitionSpec as P

H = 12.0
F32 = jnp.float32


def iota(axis, shape):
    return lax.broadcasted_iota(jnp.int32, shape, axis)


def next_z(v):
    n = v.shape[1]
    return jnp.where(iota(1, v.shape) == n - 1, 0.0, pltpu.roll(v, n - 1, 1))


def prev_z(v):
    return jnp.where(iota(1, v.shape) == 0, 0.0, pltpu.roll(v, 1, 1))


def next_y(v, row):
    n = v.shape[0]
    return jnp.where(iota(0, v.shape) == n - 1, row, pltpu.roll(v, n - 1, 0))


def prev_y(v, row):
    return jnp.where(iota(0, v.shape) == 0, row, pltpu.roll(v, 1, 0))


def strides(n):
    out = []
    s = 1
    while s < n:
        out.append(s)
        s *= 2
    return out


def reduce_factors(a, b, c, axis, store):
    n = a.shape[axis]
    for level, s in enumerate(strides(n)):
        inv = 1.0 / b
        ka = -a * pltpu.roll(inv, s, axis)
        kc = -c * pltpu.roll(inv, n - s, axis)
        store(level, ka, kc)
        b = b + ka * pltpu.roll(c, s, axis) + kc * pltpu.roll(a, n - s, axis)
        a = ka * pltpu.roll(a, s, axis)
        c = kc * pltpu.roll(c, n - s, axis)
    return 1.0 / b


def reduce_apply(r, axis, load, inv):
    n = r.shape[axis]
    for level, s in enumerate(strides(n)):
        ka, kc = load(level)
        r = r + ka * pltpu.roll(r, s, axis) + kc * pltpu.roll(r, n - s, axis)
    return r * inv


def sweep_x(rhs, xf, out):
    nx = len(rhs)
    fwd = [rhs[0]]
    for i in range(1, nx):
        fwd.append(rhs[i] + xf[0, i] * fwd[i - 1])
    u = xf[1, nx - 1] * fwd[nx - 1]
    out[nx - 1] = u
    for i in range(nx - 2, -1, -1):
        u = xf[1, i] * fwd[i] + xf[2, i] * u
        out[i] = u


def interface_factors(coef, own, n, k, weights, consts):
    zero = jnp.zeros_like(own[0])
    bs = []
    ds = []
    B = zero
    for j in range(n - 1):
        al, be, de = coef(j)
        g = be / (1.0 - al * B)
        weights[j] = g
        bs.append(B)
        B = jnp.where(j < k, de + g * be * B, B)
    D = zero
    for j in range(n - 1, 0, -1):
        al, be, de = coef(j)
        g = be / (1.0 - de * D)
        weights[j] = jnp.where(j > k, g, weights[j]) if j < n - 1 else g
        ds.append(D)
        D = jnp.where(j > k, al + g * be * D, D)
    ds.append(zero)
    ds = ds[::-1]
    al, be, de = own
    den = 1.0 / (1.0 - al * B)
    gl = be * den
    bp = de + gl * be * B
    consts[0] = gl * B
    consts[1] = be * D / (1.0 - de * D)
    consts[2] = gl
    consts[3] = bp
    consts[4] = 1.0 / (1.0 - bp * D)
    consts[5] = D
    consts[6] = den
    consts[7] = den * al
    consts[8] = B
    return bs, ds


def to_right(f, l, consts):
    return l + consts[0] * f


def to_left(f, l, consts):
    return f + consts[1] * l


def boundary(A, C, f, l, consts):
    v = (to_right(f, l, consts) + consts[2] * A + consts[3] * C) * consts[4]
    upper = C + consts[5] * v
    first = consts[6] * f + consts[7] * A + consts[2] * upper
    lower = A + consts[8] * first
    return lower, upper


def gather_sums(recv, weights, n, k):
    A = jnp.zeros_like(recv[0])
    for j in range(n - 1):
        A = jnp.where(j < k, recv[j] + weights[j] * A, A)
    C = jnp.zeros_like(A)
    for j in range(n - 1, 0, -1):
        C = jnp.where(j > k, recv[j] + weights[j] * C, C)
    return A, C


def fill_send(send, f, l, consts, n, k):
    right = to_right(f, l, consts)
    left = to_left(f, l, consts)
    for j in range(n):
        send[j] = jnp.where(j > k, right, left)


def coef_kernel(nxd, nyd, mat, perm, cond, dm, cp, yk, yib, phy, psy, xf, phx, psx, cy, cx, sendy):
    kx = lax.axis_index("gx")
    ky = lax.axis_index("gy")
    nx, ny, nz = mat.shape
    row = iota(0, (ny, nz))
    for x in range(nx):
        m = mat[x]
        eps = jnp.full(m.shape, perm[0], F32)
        sig = jnp.full(m.shape, cond[0], F32)
        for t in range(1, perm.shape[0]):
            eps = jnp.where(m == t, perm[t], eps)
            sig = jnp.where(m == t, cond[t], sig)
        ea = eps / H
        sh = sig * 0.5
        inv = 1.0 / (ea + sh)
        cp[x] = inv
        dm[x] = (ea - sh) * inv
        s = H * inv
        first = row == 0
        last = row == ny - 1
        a = jnp.where(first, 0.0, -s)
        c = jnp.where(last, 0.0, -s)
        edge = jnp.where(ky == 0, 1.0, 2.0)
        b = 1.0 + s * jnp.where(first, edge, 2.0)

        def store(level, ka, kc):
            yk[2 * level, x] = ka
            yk[2 * level + 1, x] = kc

        def load(level):
            return yk[2 * level, x], yk[2 * level + 1, x]

        ib = reduce_factors(a, b, c, 0, store)
        yib[x] = ib
        lo = reduce_apply(jnp.where(first, jnp.where(ky == 0, 0.0, s), 0.0), 0, load, ib)
        up = reduce_apply(jnp.where(last, jnp.where(ky == nyd - 1, 0.0, s), 0.0), 0, load, ib)
        phy[x] = lo
        psy[x] = up
        cy[0, x:x + 1] = lo[0:1]
        cy[1, x:x + 1] = up[0:1]
        cy[2, x:x + 1] = up[ny - 1:ny]
    for j in range(nyd):
        sendy[j] = cy[...]
    s = H * cp[0]
    d = 1.0 + s * jnp.where(kx == 0, 1.0, 2.0)
    r = jnp.where(kx == 0, 0.0, s)
    phx[0] = r
    xf[0, 0] = jnp.zeros_like(s)
    for x in range(nx):
        e = 1.0 / d
        xf[1, x] = e
        xf[2, x] = s * e
        if x < nx - 1:
            sn = H * cp[x + 1]
            p = sn * e
            xf[0, x + 1] = p
            d = 1.0 + 2.0 * sn - p * s
            r = p * r
            phx[x + 1] = r
            s = sn
    u = xf[1, nx - 1] * r
    w = jnp.where(kx == nxd - 1, 0.0, xf[2, nx - 1])
    phx[nx - 1] = u
    psx[nx - 1] = w
    cx[2] = w
    for x in range(nx - 2, -1, -1):
        u = xf[1, x] * phx[x] + xf[2, x] * u
        w = xf[2, x] * w
        phx[x] = u
        psx[x] = w
    cx[0] = u
    cx[1] = w


def zfactor_kernel(cp, zk, zib):
    nx, ny, nz = cp.shape
    lane = iota(1, (ny, nz))
    for x in range(nx):
        s = H * cp[x]
        a = jnp.where(lane == 0, 0.0, -s)
        c = jnp.where(lane == nz - 1, 0.0, -s)
        b = 1.0 + s * jnp.where(lane == 0, 1.0, 2.0)

        def store(level, ka, kc):
            zk[2 * level, x] = ka
            zk[2 * level + 1, x] = kc

        zib[x] = reduce_factors(a, b, c, 1, store)


def z_load(zk, x):
    return lambda level: (zk[2 * level, x], zk[2 * level + 1, x])


def chain_x_kernel(el, mg, dm, cp, yk, yib, e1_up, iz_out, up_out, f_out, l_out):
    nx, ny, nz = dm.shape
    for x in range(nx):
        above = el[1, x + 1] if x < nx - 1 else e1_up[0]
        iz = mg[2, x] - H * (above - el[1, x])
        iz_out[x] = iz
        h1 = mg[1, x]
        rhs = dm[x] * el[0, x] + cp[x] * ((iz - prev_y(iz, 0.0)) - (h1 - prev_z(h1)))
        u = reduce_apply(rhs, 0, z_load(yk, x), yib[x])
        up_out[x] = u
        f_out[x:x + 1] = u[0:1]
        l_out[x:x + 1] = u[ny - 1:ny] - iz[ny - 1:ny] * (1.0 / H)


def chain_z_kernel(nxd, el, mg, dm, cp, xf, cx, h0_low, iy_out, up_out, send):
    nx, ny, nz = dm.shape
    rhs = []
    below = jnp.zeros((ny, nz), F32)
    for x in range(nx):
        e0 = el[0, x]
        iy = mg[1, x] - H * (next_z(e0) - e0)
        iy_out[x] = iy
        h0 = mg[0, x]
        rhs.append(dm[x] * el[2, x] + cp[x] * ((iy - below) - (h0 - prev_y(h0, h0_low[x]))))
        below = iy
    sweep_x(rhs, xf, up_out)
    f = up_out[0]
    l = up_out[nx - 1] - below * (1.0 / H)
    for j in range(nxd):
        send[j, 0] = cx[0]
        send[j, 1] = cx[1]
        send[j, 2] = cx[2]
        send[j, 3] = f
        send[j, 4] = l


def center_y_kernel(el, mg, dm, cp, zk, zib, e2_up, h2_low, sx_out, t1_out):
    nx, ny, nz = dm.shape
    for x in range(nx):
        e2 = el[2, x]
        ix = mg[0, x] - H * (next_y(e2, e2_up[x]) - e2)
        below = mg[2, x - 1] if x > 0 else h2_low[0]
        rhs = dm[x] * el[1, x] + cp[x] * ((ix - prev_z(ix)) - (mg[2, x] - below))
        cy = reduce_apply(rhs, 1, z_load(zk, x), zib[x])
        curl = H * (next_z(cy) - cy)
        mx = ix + curl
        sx_out[x] = mx + curl
        t1_out[x] = dm[x] * cy + cp[x] * (mx - prev_z(mx))


def scan_y_kernel(recv, own, f, l, weights, consts, send):
    ky = lax.axis_index("gy")
    n = recv.shape[0]
    interface_factors(lambda j: (recv[j, 0], recv[j, 1], recv[j, 2]), (own[0], own[1], own[2]), n, ky, weights, consts)
    fill_send(send, f[...], l[...], consts, n, ky)


def half_x_kernel(recv, weights, consts, f, l, up, iz, t1, dm, cp, phy, psy, xf, sz_out, t4_out, ufy_out, f_out, l_out, edge):
    ky = lax.axis_index("gy")
    nx, ny, nz = dm.shape
    n = recv.shape[0]
    A, C = gather_sums(recv, weights, n, ky)
    lower, upper = boundary(A, C, f[...], l[...], consts)
    edge[0] = lower
    edge[1] = upper
    rhs = []
    below = jnp.zeros((ny, nz), F32)
    for x in range(nx):
        lo = edge[0, x:x + 1]
        hi = edge[1, x:x + 1]
        cx = up[x] + phy[x] * lo + psy[x] * hi
        curl = H * (next_y(cx, hi) - cx)
        mz = iz[x] + curl
        sz = mz + curl
        sz_out[x] = sz
        mlow = jnp.where(ky == 0, 0.0, H * (cx[0:1] - lo))
        t4_out[x] = dm[x] * cx + cp[x] * (mz - prev_y(mz, mlow))
        rhs.append(t1[x] - cp[x] * (sz - below))
        below = sz
    sweep_x(rhs, xf, ufy_out)
    f_out[...] = ufy_out[0]
    l_out[...] = ufy_out[nx - 1] + below * (1.0 / H)


def scan_x_kernel(recv, own, f1, l1, f2, l2, weights, consts, edge, send):
    kx = lax.axis_index("gx")
    n = recv.shape[0]
    bs, ds = interface_factors(lambda j: (recv[j, 0], recv[j, 1], recv[j, 2]), (own[0], own[1], own[2]), n, kx, weights, consts)
    fill_send(send, f2[...], l2[...], consts, n, kx)
    A = jnp.zeros(f1.shape, F32)
    for j in range(n - 1):
        A = jnp.where(j < kx, recv[j, 4] + weights[j] * (A + bs[j] * recv[j, 3]), A)
    C = jnp.zeros(f1.shape, F32)
    for j in range(n - 1, 0, -1):
        C = jnp.where(j > kx, recv[j, 3] + weights[j] * (C + ds[j] * recv[j, 4]), C)
    lower, upper = boundary(A, C, f1[...], l1[...], consts)
    edge[0] = lower
    edge[1] = upper


def half_z_kernel(edge, up, iy, sx, dm, cp, phx, psx, yk, yib, consts_y, sy_out, ufz_out, f_out, l_out, send):
    kx = lax.axis_index("gx")
    ky = lax.axis_index("gy")
    nx, ny, nz = dm.shape
    lower = edge[0]
    upper = edge[1]
    cz = up[0] + phx[0] * lower + psx[0] * upper
    below = jnp.where(kx == 0, 0.0, H * (cz - lower))
    for x in range(nx):
        cn = up[x + 1] + phx[x + 1] * lower + psx[x + 1] * upper if x < nx - 1 else upper
        curl = H * (cn - cz)
        my = iy[x] + curl
        sy_out[x] = my + curl
        s = sx[x]
        rhs = dm[x] * cz + cp[x] * ((my - below) - (s - prev_y(s, 0.0)))
        u = reduce_apply(rhs, 0, z_load(yk, x), yib[x])
        ufz_out[x] = u
        f_out[x:x + 1] = u[0:1]
        l_out[x:x + 1] = u[ny - 1:ny] + s[ny - 1:ny] * (1.0 / H)
        cz = cn
        below = my
    fill_send(send, f_out[...], l_out[...], consts_y, send.shape[0], ky)


def final_x_kernel(t4, sy, cp, zk, zib, fx_out, my_out):
    nx, ny, nz = cp.shape
    for x in range(nx):
        s = sy[x]
        fx = reduce_apply(t4[x] - cp[x] * (s - prev_z(s)), 1, z_load(zk, x), zib[x])
        fx_out[x] = fx
        my_out[x] = s - H * (next_z(fx) - fx)


def final_y_kernel(recv, weights, consts, f, l, up, sz, phx, psx, fy_out, mz_out):
    kx = lax.axis_index("gx")
    nx = up.shape[0]
    A, C = gather_sums(recv, weights, recv.shape[0], kx)
    lower, upper = boundary(A, C, f[...], l[...], consts)
    fy = up[0] + phx[0] * lower + psx[0] * upper
    for x in range(nx):
        fn = up[x + 1] + phx[x + 1] * lower + psx[x + 1] * upper if x < nx - 1 else upper
        fy_out[x] = fy
        mz_out[x] = sz[x] - H * (fn - fy)
        fy = fn


def final_z_kernel(recv, weights, consts, f, l, up, sx, phy, psy, fx, fy, my, mz, e_out, h_out, edge):
    ky = lax.axis_index("gy")
    nx = up.shape[0]
    A, C = gather_sums(recv, weights, recv.shape[0], ky)
    lower, upper = boundary(A, C, f[...], l[...], consts)
    edge[0] = lower
    edge[1] = upper
    for x in range(nx):
        lo = edge[0, x:x + 1]
        hi = edge[1, x:x + 1]
        fz = up[x] + phy[x] * lo + psy[x] * hi
        e_out[0, x] = fx[x]
        e_out[1, x] = fy[x]
        e_out[2, x] = fz
        h_out[0, x] = sx[x] - H * (next_y(fz, hi) - fz)
        h_out[1, x] = my[x]
        h_out[2, x] = mz[x]


def vmem():
    return pl.BlockSpec(memory_space=pltpu.VMEM)


def call(kernel, outs, *args, smem=(), scratch=(), name=None):
    specs = [pl.BlockSpec(memory_space=pltpu.SMEM) if i in smem else vmem() for i in range(len(args))]
    nbytes = sum(a.size * 4 for a in args) + sum(4 * _size(o) for o in outs)
    return pl.pallas_call(
        kernel,
        out_shape=[jax.ShapeDtypeStruct(o, F32) for o in outs],
        in_specs=specs,
        out_specs=[vmem() for _ in outs],
        scratch_shapes=list(scratch),
        cost_estimate=pl.CostEstimate(flops=4 * nbytes, bytes_accessed=nbytes, transcendentals=0),
        compiler_params=pltpu.CompilerParams(vmem_limit_bytes=40 << 20),
        name=name,
    )(*args)


def _size(shape):
    n = 1
    for d in shape:
        n *= d
    return n


def shifted(array, axis, by):
    count = lax.axis_size(axis)
    return lax.ppermute(array, axis, [(i, i + by) for i in range(count) if 0 <= i + by < count])


def exchange(array, axis):
    return lax.all_to_all(array, axis, 0, 0)


def per_device(electric, magnetic, material, permittivity, conductivity):
    nxd = lax.axis_size("gx")
    nyd = lax.axis_size("gy")
    cell = material.shape
    nx, ny, nz = cell
    py = (nx, nz)
    px = (ny, nz)

    def bind(kernel, *lead):
        def body(*refs):
            kernel(*lead, *refs)
        return body

    dm, cp, yk, yib, phy, psy, xf, phx, psx, cy, cx, sendy = call(
        bind(coef_kernel, nxd, nyd),
        [cell, cell, (2 * len(strides(ny)),) + cell, cell, cell, cell, (3,) + cell, cell, cell,
         (3,) + py, (3,) + px, (nyd, 3) + py],
        material, permittivity, conductivity, smem=(1, 2), name="coef")
    recv_cy = exchange(sendy, "gy")

    e1_up = shifted(electric[1, 0:1], "gx", -1)
    h0_low = shifted(magnetic[0, :, ny - 1:ny], "gy", 1)
    e2_up = shifted(electric[2, :, 0:1], "gy", -1)
    h2_low = shifted(magnetic[2, nx - 1:nx], "gx", 1)

    zk, zib = call(zfactor_kernel, [(2 * len(strides(nz)),) + cell, cell], cp, name="zfactor")
    iz, ux, fx1, lx1 = call(chain_x_kernel, [cell, cell, py, py], electric, magnetic, dm, cp, yk, yib, e1_up, name="chain_x")
    wy, ky, send = call(scan_y_kernel, [(nyd,) + py, (9,) + py, (nyd,) + py], recv_cy, cy, fx1, lx1, name="scan_y")
    recv1 = exchange(send, "gy")

    iy, uz, sendx = call(bind(chain_z_kernel, nxd), [cell, cell, (nxd, 5) + px], electric, magnetic, dm, cp, xf, cx, h0_low, name="chain_z")
    recv2 = exchange(sendx, "gx")
    sx, t1 = call(center_y_kernel, [cell, cell], electric, magnetic, dm, cp, zk, zib, e2_up, h2_low, name="center_y")

    sz, t4, ufy, f3, l3 = call(half_x_kernel, [cell, cell, cell, px, px],
                               recv1, wy, ky, fx1, lx1, ux, iz, t1, dm, cp, phy, psy, xf,
                               scratch=[pltpu.VMEM((2,) + py, F32)], name="half_x")
    fz2 = sendx[0, 3]
    lz2 = sendx[0, 4]
    wx, kx, edge2, send3 = call(scan_x_kernel, [(nxd,) + px, (9,) + px, (2,) + px, (nxd,) + px],
                                recv2, cx, fz2, lz2, f3, l3, name="scan_x")
    recv3 = exchange(send3, "gx")
    sy, ufz, f4, l4, send4 = call(half_z_kernel, [cell, cell, py, py, (nyd,) + py],
                                  edge2, uz, iy, sx, dm, cp, phx, psx, yk, yib, ky, name="half_z")
    recv4 = exchange(send4, "gy")
    fx, my = call(final_x_kernel, [cell, cell], t4, sy, cp, zk, zib, name="final_x")
    fy, mz = call(final_y_kernel, [cell, cell], recv3, wx, kx, f3, l3, ufy, sz, phx, psx, name="final_y")
    e, h = call(final_z_kernel, [(3,) + cell, (3,) + cell],
                recv4, wy, ky, f4, l4, ufz, sx, phy, psy, fx, fy, my, mz,
                scratch=[pltpu.VMEM((2,) + py, F32)], name="final_z")
    return e, h


def solution(mesh):
    return jax.shard_map(
        per_device,
        mesh=mesh,
        in_specs=(
            P(None, "gx", "gy", None),
            P(None, "gx", "gy", None),
            P("gx", "gy", None),
            P(),
            P(),
        ),
        out_specs=(P(None, "gx", "gy", None), P(None, "gx", "gy", None)),
        check_vma=False,
    )
```

```python
import jax
import jax.numpy as jnp
from jax import lax
from jax.experimental import pallas as pl
from jax.experimental.pallas import tpu as pltpu
from jax.sharding import PartitionSpec as P

H = 12.0
F32 = jnp.float32
HBM = pltpu.HBM


def iota(axis, shape):
    return lax.broadcasted_iota(jnp.int32, shape, axis)


def next_z(v):
    n = v.shape[1]
    return jnp.where(iota(1, v.shape) == n - 1, 0.0, pltpu.roll(v, n - 1, 1))


def prev_z(v):
    return jnp.where(iota(1, v.shape) == 0, 0.0, pltpu.roll(v, 1, 1))


def next_y(v, row):
    n = v.shape[0]
    return jnp.where(iota(0, v.shape) == n - 1, row, pltpu.roll(v, n - 1, 0))


def prev_y(v, row):
    return jnp.where(iota(0, v.shape) == 0, row, pltpu.roll(v, 1, 0))


def strides(n):
    out = []
    s = 1
    while s < n:
        out.append(s)
        s *= 2
    return out


def reduce_factors(a, b, c, axis, store):
    n = a.shape[axis]
    for level, s in enumerate(strides(n)):
        inv = 1.0 / b
        ka = -a * pltpu.roll(inv, s, axis)
        kc = -c * pltpu.roll(inv, n - s, axis)
        store(level, ka, kc)
        b = b + ka * pltpu.roll(c, s, axis) + kc * pltpu.roll(a, n - s, axis)
        a = ka * pltpu.roll(a, s, axis)
        c = kc * pltpu.roll(c, n - s, axis)
    return 1.0 / b


def reduce_apply(r, axis, load, inv):
    n = r.shape[axis]
    for level, s in enumerate(strides(n)):
        ka, kc = load(level)
        r = r + ka * pltpu.roll(r, s, axis) + kc * pltpu.roll(r, n - s, axis)
    return r * inv


def sweep_x(rhs, xf, out):
    nx = len(rhs)
    fwd = [rhs[0]]
    for i in range(1, nx):
        fwd.append(rhs[i] + xf[0, i] * fwd[i - 1])
    u = xf[1, nx - 1] * fwd[nx - 1]
    out[nx - 1] = u
    for i in range(nx - 2, -1, -1):
        u = xf[1, i] * fwd[i] + xf[2, i] * u
        out[i] = u


def interface_factors(coef, own, n, k, weights, mixed, consts):
    zero = jnp.zeros_like(own[0])
    B = zero
    for j in range(n - 1):
        al, be, de = coef(j)
        g = be / (1.0 - al * B)
        h = g * B
        weights[j] = g
        mixed[j] = h
        B = jnp.where(j < k, de + h * be, B)
    D = zero
    for j in range(n - 1, 0, -1):
        al, be, de = coef(j)
        g = be / (1.0 - de * D)
        h = g * D
        weights[j] = jnp.where(j > k, g, weights[j]) if j < n - 1 else g
        mixed[j] = jnp.where(j > k, h, mixed[j]) if j < n - 1 else h
        D = jnp.where(j > k, al + h * be, D)
    al, be, de = own
    den = 1.0 / (1.0 - al * B)
    gl = be * den
    bp = de + gl * be * B
    consts[0] = gl * B
    consts[1] = be * D / (1.0 - de * D)
    consts[2] = gl
    consts[3] = bp
    consts[4] = 1.0 / (1.0 - bp * D)
    consts[5] = D
    consts[6] = den
    consts[7] = den * al
    consts[8] = B


def to_right(f, l, consts):
    return l + consts[0] * f


def to_left(f, l, consts):
    return f + consts[1] * l


def boundary(A, C, f, l, consts):
    v = (to_right(f, l, consts) + consts[2] * A + consts[3] * C) * consts[4]
    upper = C + consts[5] * v
    first = consts[6] * f + consts[7] * A + consts[2] * upper
    lower = A + consts[8] * first
    return lower, upper


def gather_sums(recv, weights, n, k):
    A = jnp.zeros_like(recv[0])
    for j in range(n - 1):
        A = jnp.where(j < k, recv[j] + weights[j] * A, A)
    C = jnp.zeros_like(A)
    for j in range(n - 1, 0, -1):
        C = jnp.where(j > k, recv[j] + weights[j] * C, C)
    return A, C


def gather_sums_pair(pair, weights, mixed, n, k):
    A = jnp.zeros_like(weights[0])
    for j in range(n - 1):
        f, l = pair(j)
        A = jnp.where(j < k, l + mixed[j] * f + weights[j] * A, A)
    C = jnp.zeros_like(A)
    for j in range(n - 1, 0, -1):
        f, l = pair(j)
        C = jnp.where(j > k, f + mixed[j] * l + weights[j] * C, C)
    return A, C


def fill_send(send, f, l, consts, n, k):
    right = to_right(f, l, consts)
    left = to_left(f, l, consts)
    for j in range(n):
        send[j] = jnp.where(j > k, right, left)


def coef_kernel(nxd, nyd, mat, perm, cond, dm, cp, yk, yib, phy, psy, xf, phx, psx, cy, cx):
    kx = lax.axis_index("gx")
    ky = lax.axis_index("gy")
    nx, ny, nz = mat.shape
    row = iota(0, (ny, nz))
    for x in range(nx):
        m = mat[x]
        eps = jnp.full(m.shape, perm[0], F32)
        sig = jnp.full(m.shape, cond[0], F32)
        for t in range(1, perm.shape[0]):
            eps = jnp.where(m == t, perm[t], eps)
            sig = jnp.where(m == t, cond[t], sig)
        ea = eps / H
        sh = sig * 0.5
        inv = 1.0 / (ea + sh)
        cp[x] = inv
        dm[x] = (ea - sh) * inv
        s = H * inv
        first = row == 0
        last = row == ny - 1
        a = jnp.where(first, 0.0, -s)
        c = jnp.where(last, 0.0, -s)
        edge = jnp.where(ky == 0, 1.0, 2.0)
        b = 1.0 + s * jnp.where(first, edge, 2.0)

        def store(level, ka, kc):
            yk[2 * level, x] = ka
            yk[2 * level + 1, x] = kc

        def load(level):
            return yk[2 * level, x], yk[2 * level + 1, x]

        ib = reduce_factors(a, b, c, 0, store)
        yib[x] = ib
        lo = reduce_apply(jnp.where(first, jnp.where(ky == 0, 0.0, s), 0.0), 0, load, ib)
        up = reduce_apply(jnp.where(last, jnp.where(ky == nyd - 1, 0.0, s), 0.0), 0, load, ib)
        phy[x] = lo
        psy[x] = up
        cy[0, x:x + 1] = lo[0:1]
        cy[1, x:x + 1] = up[0:1]
        cy[2, x:x + 1] = up[ny - 1:ny]
    s = H * cp[0]
    d = 1.0 + s * jnp.where(kx == 0, 1.0, 2.0)
    r = jnp.where(kx == 0, 0.0, s)
    phx[0] = r
    xf[0, 0] = jnp.zeros_like(s)
    for x in range(nx):
        e = 1.0 / d
        xf[1, x] = e
        xf[2, x] = s * e
        if x < nx - 1:
            sn = H * cp[x + 1]
            p = sn * e
            xf[0, x + 1] = p
            d = 1.0 + 2.0 * sn - p * s
            r = p * r
            phx[x + 1] = r
            s = sn
    u = xf[1, nx - 1] * r
    w = jnp.where(kx == nxd - 1, 0.0, xf[2, nx - 1])
    phx[nx - 1] = u
    psx[nx - 1] = w
    cx[2] = w
    for x in range(nx - 2, -1, -1):
        u = xf[1, x] * phx[x] + xf[2, x] * u
        w = xf[2, x] * w
        phx[x] = u
        psx[x] = w
    cx[0] = u
    cx[1] = w


def zfactor_kernel(cp, zk, zib):
    nx, ny, nz = cp.shape
    lane = iota(1, (ny, nz))
    for x in range(nx):
        s = H * cp[x]
        a = jnp.where(lane == 0, 0.0, -s)
        c = jnp.where(lane == nz - 1, 0.0, -s)
        b = 1.0 + s * jnp.where(lane == 0, 1.0, 2.0)

        def store(level, ka, kc):
            zk[2 * level, x] = ka
            zk[2 * level + 1, x] = kc

        zib[x] = reduce_factors(a, b, c, 1, store)


def z_load(zk, x):
    return lambda level: (zk[2 * level, x], zk[2 * level + 1, x])


def chain_x_kernel(nyd, el, mg, dm, cp, yk, yib, cy, e1_up, iz_out, up_out, send, pair):
    nx, ny, nz = dm.shape
    for x in range(nx):
        above = el[1, x + 1] if x < nx - 1 else e1_up[0]
        iz = mg[2, x] - H * (above - el[1, x])
        iz_out[x] = iz
        h1 = mg[1, x]
        rhs = dm[x] * el[0, x] + cp[x] * ((iz - prev_y(iz, 0.0)) - (h1 - prev_z(h1)))
        u = reduce_apply(rhs, 0, z_load(yk, x), yib[x])
        up_out[x] = u
        pair[0, x:x + 1] = u[0:1]
        pair[1, x:x + 1] = u[ny - 1:ny] - iz[ny - 1:ny] * (1.0 / H)
    for j in range(nyd):
        send[j, 0:3] = cy[...]
        send[j, 3:5] = pair[...]


def chain_z_kernel(el, mg, dm, cp, xf, h0_low, iy_out, up_out, pair):
    nx, ny, nz = dm.shape
    rhs = []
    below = jnp.zeros((ny, nz), F32)
    for x in range(nx):
        e0 = el[0, x]
        iy = mg[1, x] - H * (next_z(e0) - e0)
        iy_out[x] = iy
        h0 = mg[0, x]
        rhs.append(dm[x] * el[2, x] + cp[x] * ((iy - below) - (h0 - prev_y(h0, h0_low[x]))))
        below = iy
    sweep_x(rhs, xf, up_out)
    pair[0] = up_out[0]
    pair[1] = up_out[nx - 1] - below * (1.0 / H)


def center_y_kernel(el, mg, dm, cp, zk, zib, e2_up, h2_low, sx_out, t1_out):
    nx, ny, nz = dm.shape
    for x in range(nx):
        e2 = el[2, x]
        ix = mg[0, x] - H * (next_y(e2, e2_up[x]) - e2)
        below = mg[2, x - 1] if x > 0 else h2_low[0]
        rhs = dm[x] * el[1, x] + cp[x] * ((ix - prev_z(ix)) - (mg[2, x] - below))
        cy = reduce_apply(rhs, 1, z_load(zk, x), zib[x])
        curl = H * (next_z(cy) - cy)
        mx = ix + curl
        sx_out[x] = mx + curl
        t1_out[x] = dm[x] * cy + cp[x] * (mx - prev_z(mx))


def half_x_kernel(nxd, ready, recv, cy, up, iz, t1, dm, cp, phy, psy, xf, coef_x, pair_z, sz_out, t4_out, ufy_out, send, weights, consts, mixed, edge):
    ky = lax.axis_index("gy")
    nx, ny, nz = dm.shape
    n = recv.shape[0]
    interface_factors(lambda j: (recv[j, 0], recv[j, 1], recv[j, 2]), (cy[0], cy[1], cy[2]), n, ky, weights, mixed, consts)
    A, C = gather_sums_pair(lambda j: (recv[j, 3], recv[j, 4]), weights, mixed, n, ky)
    ready()
    for x in range(nx):
        edge[0, x:x + 1] = up[x][0:1]
        edge[1, x:x + 1] = up[x][ny - 1:ny] - iz[x][ny - 1:ny] * (1.0 / H)
    lower, upper = boundary(A, C, edge[0], edge[1], consts)
    edge[0] = lower
    edge[1] = upper
    rhs = []
    below = jnp.zeros((ny, nz), F32)
    for x in range(nx):
        lo = edge[0, x:x + 1]
        hi = edge[1, x:x + 1]
        cx = up[x] + phy[x] * lo + psy[x] * hi
        curl = H * (next_y(cx, hi) - cx)
        mz = iz[x] + curl
        sz = mz + curl
        sz_out[x] = sz
        mlow = jnp.where(ky == 0, 0.0, H * (cx[0:1] - lo))
        t4_out[x] = dm[x] * cx + cp[x] * (mz - prev_y(mz, mlow))
        rhs.append(t1[x] - cp[x] * (sz - below))
        below = sz
    sweep_x(rhs, xf, ufy_out)
    f = ufy_out[0]
    l = ufy_out[nx - 1] + below * (1.0 / H)
    for j in range(nxd):
        for i in range(3):
            send[j, i] = coef_x[i]
        send[j, 3] = pair_z[0]
        send[j, 4] = pair_z[1]
        send[j, 5] = f
        send[j, 6] = l


def half_z_kernel(ready, recv, cx, pair_z, up, iy, sx, ufy, sz, dm, cp, phx, psx, yk, yib, consts_y, sy_out, ufz_out, pair_out, edge_y_out, send, weights, mixed, consts):
    kx = lax.axis_index("gx")
    ky = lax.axis_index("gy")
    nx, ny, nz = dm.shape
    n = recv.shape[0]
    interface_factors(lambda j: (recv[j, 0], recv[j, 1], recv[j, 2]), (cx[0], cx[1], cx[2]), n, kx, weights, mixed, consts)
    A, C = gather_sums_pair(lambda j: (recv[j, 5], recv[j, 6]), weights, mixed, n, kx)
    ready()
    lower, upper = boundary(A, C, ufy[0], ufy[nx - 1] + sz[nx - 1] * (1.0 / H), consts)
    edge_y_out[0] = lower
    edge_y_out[1] = upper
    A, C = gather_sums_pair(lambda j: (recv[j, 3], recv[j, 4]), weights, mixed, n, kx)
    lower, upper = boundary(A, C, pair_z[0], pair_z[1], consts)
    cz = up[0] + phx[0] * lower + psx[0] * upper
    below = jnp.where(kx == 0, 0.0, H * (cz - lower))
    for x in range(nx):
        cn = up[x + 1] + phx[x + 1] * lower + psx[x + 1] * upper if x < nx - 1 else upper
        curl = H * (cn - cz)
        my = iy[x] + curl
        sy_out[x] = my + curl
        s = sx[x]
        rhs = dm[x] * cz + cp[x] * ((my - below) - (s - prev_y(s, 0.0)))
        u = reduce_apply(rhs, 0, z_load(yk, x), yib[x])
        ufz_out[x] = u
        pair_out[0, x:x + 1] = u[0:1]
        pair_out[1, x:x + 1] = u[ny - 1:ny] + s[ny - 1:ny] * (1.0 / H)
        cz = cn
        below = my
    fill_send(send, pair_out[0], pair_out[1], consts_y, send.shape[0], ky)


def final_x_kernel(t4, sy, cp, zk, zib, fx_out, my_out):
    nx, ny, nz = cp.shape
    for x in range(nx):
        s = sy[x]
        fx = reduce_apply(t4[x] - cp[x] * (s - prev_z(s)), 1, z_load(zk, x), zib[x])
        fx_out[x] = fx
        my_out[x] = s - H * (next_z(fx) - fx)


def final_y_kernel(edge, up, sz, phx, psx, fy_out, mz_out):
    nx = up.shape[0]
    lower = edge[0]
    upper = edge[1]
    fy = up[0] + phx[0] * lower + psx[0] * upper
    for x in range(nx):
        fn = up[x + 1] + phx[x + 1] * lower + psx[x + 1] * upper if x < nx - 1 else upper
        fy_out[x] = fy
        mz_out[x] = sz[x] - H * (fn - fy)
        fy = fn


def final_z_kernel(ready, recv, weights, consts, pair, up, sx, phy, psy, fx, fy, my, mz, e_out, h_out, edge):
    ky = lax.axis_index("gy")
    nx = up.shape[0]
    A, C = gather_sums(recv, weights, recv.shape[0], ky)
    lower, upper = boundary(A, C, pair[0], pair[1], consts)
    ready()
    edge[0] = lower
    edge[1] = upper
    for x in range(nx):
        lo = edge[0, x:x + 1]
        hi = edge[1, x:x + 1]
        fz = up[x] + phy[x] * lo + psy[x] * hi
        e_out[0, x] = fx[x]
        e_out[1, x] = fy[x]
        e_out[2, x] = fz
        h_out[0, x] = sx[x] - H * (next_y(fz, hi) - fz)
        h_out[1, x] = my[x]
        h_out[2, x] = mz[x]


def staged(kernel, kinds_in, kinds_out, first):
    def body(*refs):
        ni = len(kinds_in)
        no = len(kinds_out)
        ins = refs[:ni]
        outs = refs[ni:ni + no]
        rest = list(refs[ni + no:])
        sems = rest.pop()
        work = []
        copies = []
        for ref, kind in zip(ins, kinds_in):
            if kind == "v":
                work.append(ref)
                continue
            held = rest.pop(0)
            copy = pltpu.make_async_copy(ref, held, sems.at[len(copies)])
            copy.start()
            copies.append(copy)
            work.append(held)
        back = []
        for ref, kind in zip(outs, kinds_out):
            if kind == "v":
                work.append(ref)
                continue
            held = rest.pop(0)
            back.append((held, ref))
            work.append(held)
        head = len(copies) if first is None else first
        for copy in copies[:head]:
            copy.wait()

        def ready():
            for copy in copies[head:]:
                copy.wait()

        if first is None:
            kernel(*work, *rest)
        else:
            kernel(ready, *work, *rest)
        copies = [pltpu.make_async_copy(held, ref, sems.at[i]) for i, (held, ref) in enumerate(back)]
        for copy in copies:
            copy.start()
        for copy in copies:
            copy.wait()

    return body


def call(kernel, outs, *args, smem=(), near=(), near_out=(), scratch=(), first=None, name=None):
    kinds_in = ["s" if i in smem else "v" if i in near else "h" for i in range(len(args))]
    kinds_out = ["v" if i in near_out else "h" for i in range(len(outs))]
    held = []
    for a, kind in zip(args, kinds_in):
        if kind != "v":
            held.append((pltpu.SMEM if kind == "s" else pltpu.VMEM)(a.shape, a.dtype))
    for o, kind in zip(outs, kinds_out):
        if kind != "v":
            held.append(pltpu.VMEM(o, F32))
    spec = {"v": pltpu.VMEM, "h": HBM, "s": HBM}
    nbytes = sum(4 * _size(a.shape) for a in args) + sum(4 * _size(o) for o in outs)
    return pl.pallas_call(
        staged(kernel, kinds_in, kinds_out, first),
        out_shape=[jax.ShapeDtypeStruct(o, F32) for o in outs],
        in_specs=[pl.BlockSpec(memory_space=spec[k]) for k in kinds_in],
        out_specs=[pl.BlockSpec(memory_space=spec[k]) for k in kinds_out],
        scratch_shapes=held + list(scratch) + [pltpu.SemaphoreType.DMA((len(held),))],
        cost_estimate=pl.CostEstimate(flops=4 * nbytes, bytes_accessed=nbytes, transcendentals=0),
        compiler_params=pltpu.CompilerParams(vmem_limit_bytes=60 << 20),
        name=name,
    )(*args)


def _size(shape):
    n = 1
    for d in shape:
        n *= d
    return n


def shifted(array, axis, by):
    count = lax.axis_size(axis)
    return lax.ppermute(array, axis, [(i, i + by) for i in range(count) if 0 <= i + by < count])


def exchange(array, axis):
    return lax.all_to_all(array, axis, 0, 0)


def per_device(electric, magnetic, material, permittivity, conductivity):
    nxd = lax.axis_size("gx")
    nyd = lax.axis_size("gy")
    cell = material.shape
    nx, ny, nz = cell
    py = (nx, nz)
    px = (ny, nz)

    def bind(kernel, *lead):
        def body(*refs):
            kernel(*lead, *refs)
        return body


    dm, cp, yk, yib, phy, psy, xf, phx, psx, cy, cx = call(
        bind(coef_kernel, nxd, nyd),
        [cell, cell, (2 * len(strides(ny)),) + cell, cell, cell, cell, (3,) + cell, cell, cell, (3,) + py, (3,) + px],
        material, permittivity, conductivity, smem=(1, 2), name="coef")
    e1_up = shifted(lax.optimization_barrier((electric[1, 0:1], cx))[0], "gx", -1)
    iz, ux, send1 = call(bind(chain_x_kernel, nyd), [cell, cell, (nyd, 5) + py],
                         electric, magnetic, dm, cp, yk, yib, cy, e1_up, scratch=[pltpu.VMEM((2,) + py, F32)], name="chain_x")
    recv1 = exchange(send1, "gy")

    h0_low = shifted(magnetic[0, :, ny - 1:ny], "gy", 1)
    e2_up = shifted(electric[2, :, 0:1], "gy", -1)
    h2_low = shifted(magnetic[2, nx - 1:nx], "gx", 1)
    zk, zib = call(zfactor_kernel, [(2 * len(strides(nz)),) + cell, cell], cp, name="zfactor")
    iy, uz, pair_z = call(chain_z_kernel, [cell, cell, (2,) + px], electric, magnetic, dm, cp, xf, h0_low, name="chain_z")
    sx, t1 = call(center_y_kernel, [cell, cell], electric, magnetic, dm, cp, zk, zib, e2_up, h2_low, name="center_y")

    sz, t4, ufy, send2, wy, ky = call(
        bind(half_x_kernel, nxd), [cell, cell, cell, (nxd, 7) + px, (nyd,) + py, (9,) + py],
        recv1, cy, ux, iz, t1, dm, cp, phy, psy, xf, cx, pair_z,
        first=2, scratch=[pltpu.VMEM((nyd,) + py, F32), pltpu.VMEM((2,) + py, F32)], name="half_x")
    recv2 = exchange(send2, "gx")
    sy, ufz, pair4, edge_y, send3 = call(
        half_z_kernel, [cell, cell, (2,) + py, (2,) + px, (nyd,) + py],
        recv2, cx, pair_z, uz, iy, sx, ufy, sz, dm, cp, phx, psx, yk, yib, ky,
        first=2, scratch=[pltpu.VMEM((nxd,) + px, F32), pltpu.VMEM((nxd,) + px, F32), pltpu.VMEM((9,) + px, F32)],
        name="half_z")
    recv3 = exchange(send3, "gy")
    fx, my = call(final_x_kernel, [cell, cell], t4, sy, cp, zk, zib, name="final_x")
    fy, mz = call(final_y_kernel, [cell, cell], edge_y, ufy, sz, phx, psx, name="final_y")
    e, h = call(final_z_kernel, [(3,) + cell, (3,) + cell],
                recv3, wy, ky, pair4, ufz, sx, phy, psy, fx, fy, my, mz,
                first=4, scratch=[pltpu.VMEM((2,) + py, F32)], name="final_z")
    return e, h


def solution(mesh):
    return jax.shard_map(
        per_device,
        mesh=mesh,
        in_specs=(
            P(None, "gx", "gy", None),
            P(None, "gx", "gy", None),
            P("gx", "gy", None),
            P(),
            P(),
        ),
        out_specs=(P(None, "gx", "gy", None), P(None, "gx", "gy", None)),
        check_vma=False,
    )
```

```python
import jax
import jax.numpy as jnp
from jax import lax
from jax.experimental import pallas as pl
from jax.experimental.pallas import tpu as pltpu
from jax.sharding import PartitionSpec as P

H = 12.0
F32 = jnp.float32
HBM = pltpu.HBM
ROOM = 60


def iota(axis, shape):
    return lax.broadcasted_iota(jnp.int32, shape, axis)


def next_z(v):
    n = v.shape[1]
    return jnp.where(iota(1, v.shape) == n - 1, 0.0, pltpu.roll(v, n - 1, 1))


def prev_z(v):
    return jnp.where(iota(1, v.shape) == 0, 0.0, pltpu.roll(v, 1, 1))


def next_y(v, row):
    n = v.shape[0]
    return jnp.where(iota(0, v.shape) == n - 1, row, pltpu.roll(v, n - 1, 0))


def prev_y(v, row):
    return jnp.where(iota(0, v.shape) == 0, row, pltpu.roll(v, 1, 0))


def strides(n):
    out = []
    s = 1
    while s < n:
        out.append(s)
        s *= 2
    return out


def reduce_factors(a, b, axis, store):
    n = a.shape[axis]
    for level, s in enumerate(strides(n)):
        inv = 1.0 / b
        c = pltpu.roll(a, n - s, axis)
        ka = -a * pltpu.roll(inv, s, axis)
        kc = -c * pltpu.roll(inv, n - s, axis)
        store(level, ka, kc)
        b = b + ka * a + kc * c
        a = ka * pltpu.roll(a, s, axis)
    return 1.0 / b


def reduce_apply(r, axis, load, inv):
    n = r.shape[axis]
    for level, s in enumerate(strides(n)):
        ka, kc = load(level)
        r = r + ka * pltpu.roll(r, s, axis) + kc * pltpu.roll(r, n - s, axis)
    return r * inv


def sweep_x(rhs, ex, out):
    nx = len(rhs)
    fwd = [rhs[0]]
    for i in range(1, nx):
        fwd.append(rhs[i] + ex[i - 1] * fwd[i - 1])
    u = ex[nx - 1] * fwd[nx - 1]
    out[nx - 1] = u
    for i in range(nx - 2, -1, -1):
        u = ex[i] * (fwd[i] + u)
        out[i] = u


def interface_factors(coef, own, n, k, weights, mixed, consts):
    zero = jnp.zeros_like(own[0])
    B = zero
    for j in range(n - 1):
        al, be, de = coef(j)
        g = be / (1.0 - al * B)
        h = g * B
        weights[j] = g
        mixed[j] = h
        B = jnp.where(j < k, de + h * be, B)
    D = zero
    for j in range(n - 1, 0, -1):
        al, be, de = coef(j)
        g = be / (1.0 - de * D)
        h = g * D
        weights[j] = jnp.where(j > k, g, weights[j]) if j < n - 1 else g
        mixed[j] = jnp.where(j > k, h, mixed[j]) if j < n - 1 else h
        D = jnp.where(j > k, al + h * be, D)
    al, be, de = own
    den = 1.0 / (1.0 - al * B)
    gl = be * den
    bp = de + gl * be * B
    consts[0] = gl * B
    consts[1] = be * D / (1.0 - de * D)
    consts[2] = gl
    consts[3] = bp
    consts[4] = 1.0 / (1.0 - bp * D)
    consts[5] = D
    consts[6] = den
    consts[7] = den * al
    consts[8] = B


def to_right(f, l, consts):
    return l + consts[0] * f


def to_left(f, l, consts):
    return f + consts[1] * l


def boundary(A, C, f, l, consts):
    v = (to_right(f, l, consts) + consts[2] * A + consts[3] * C) * consts[4]
    upper = C + consts[5] * v
    first = consts[6] * f + consts[7] * A + consts[2] * upper
    lower = A + consts[8] * first
    return lower, upper


def gather_sums(recv, weights, n, k):
    A = jnp.zeros_like(recv[0])
    for j in range(n - 1):
        A = jnp.where(j < k, recv[j] + weights[j] * A, A)
    C = jnp.zeros_like(A)
    for j in range(n - 1, 0, -1):
        C = jnp.where(j > k, recv[j] + weights[j] * C, C)
    return A, C


def gather_sums_pair(pair, weights, mixed, n, k):
    A = jnp.zeros_like(weights[0])
    for j in range(n - 1):
        f, l = pair(j)
        A = jnp.where(j < k, l + mixed[j] * f + weights[j] * A, A)
    C = jnp.zeros_like(A)
    for j in range(n - 1, 0, -1):
        f, l = pair(j)
        C = jnp.where(j > k, f + mixed[j] * l + weights[j] * C, C)
    return A, C


def fill_send(send, f, l, consts, n, k):
    right = to_right(f, l, consts)
    left = to_left(f, l, consts)
    for j in range(n):
        send[j] = jnp.where(j > k, right, left)


def coef_kernel(nyd, ready, mat, perm, cond, el, mg, ds, si, yk, yib, phy, psy, cy, send, pe1, ph2, pe2, ph0):
    ky = lax.axis_index("gy")
    nx, ny, nz = mat.shape
    row = iota(0, (ny, nz))
    for x in range(nx):
        m = mat[x]
        eps = jnp.full(m.shape, perm[0], F32)
        sig = jnp.full(m.shape, cond[0], F32)
        for t in range(1, perm.shape[0]):
            eps = jnp.where(m == t, perm[t], eps)
            sig = jnp.where(m == t, cond[t], sig)
        ea = eps * (1.0 / (H * H))
        sh = sig * (0.5 / H)
        ds[x] = ea - sh
        inv_s = ea + sh
        si[x] = inv_s
        first = row == 0
        last = row == ny - 1
        a = jnp.where(first, 0.0, jnp.full(m.shape, -1.0, F32))
        b = inv_s + jnp.where(first, jnp.where(ky == 0, 1.0, 2.0), 2.0)

        def store(level, ka, kc):
            yk[2 * level, x] = ka
            yk[2 * level + 1, x] = kc

        def load(level):
            return yk[2 * level, x], yk[2 * level + 1, x]

        ib = reduce_factors(a, b, 0, store)
        yib[x] = ib
        lo = reduce_apply(jnp.where(first, jnp.where(ky == 0, 0.0, 1.0), jnp.zeros(m.shape, F32)), 0, load, ib)
        up = reduce_apply(jnp.where(last, jnp.where(ky == nyd - 1, 0.0, 1.0), jnp.zeros(m.shape, F32)), 0, load, ib)
        phy[x] = lo
        psy[x] = up
        cy[0, x:x + 1] = lo[0:1]
        cy[1, x:x + 1] = up[0:1]
        cy[2, x:x + 1] = up[ny - 1:ny]
    for j in range(nyd):
        send[j, 0:3] = cy[...]
    ready()
    pe1[0] = el[1, 0]
    ph2[0] = mg[2, nx - 1]
    for x in range(nx):
        pe2[x:x + 1] = el[2, x][0:1]
        ph0[x:x + 1] = mg[0, x][ny - 1:ny]
    for j in range(nyd):
        send[j, 3] = jnp.where(j > ky, ph0[...], pe2[...])


def factor_kernel(nxd, si, zk, zib, ex, phx, psx, cx):
    kx = lax.axis_index("gx")
    nx, ny, nz = si.shape
    lane = iota(1, (ny, nz))
    for x in range(nx):
        a = jnp.where(lane == 0, 0.0, jnp.full((ny, nz), -1.0, F32))
        b = si[x] + jnp.where(lane == 0, 1.0, jnp.full((ny, nz), 2.0, F32))

        def store(level, ka, kc):
            zk[2 * level, x] = ka
            zk[2 * level + 1, x] = kc

        zib[x] = reduce_factors(a, b, 1, store)
    d = si[0] + jnp.where(kx == 0, 1.0, 2.0)
    r = jnp.full((ny, nz), jnp.where(kx == 0, 0.0, 1.0), F32)
    phx[0] = r
    for x in range(nx):
        e = 1.0 / d
        ex[x] = e
        if x < nx - 1:
            d = si[x + 1] + (2.0 - e)
            r = e * r
            phx[x + 1] = r
    u = ex[nx - 1] * r
    w = ex[nx - 1] * jnp.where(kx == nxd - 1, 0.0, 1.0)
    phx[nx - 1] = u
    psx[nx - 1] = w
    cx[2] = w
    for x in range(nx - 2, -1, -1):
        u = ex[x] * (phx[x] + u)
        w = ex[x] * w
        phx[x] = u
        psx[x] = w
    cx[0] = u
    cx[1] = w


def z_load(zk, x):
    return lambda level: (zk[2 * level, x], zk[2 * level + 1, x])


def chain_x_kernel(el, mg, ds, yk, yib, e1_up, iz_out, up_out, pair):
    nx, ny, nz = ds.shape
    for x in range(nx):
        above = el[1, x + 1] if x < nx - 1 else e1_up[0]
        iz = mg[2, x] - H * (above - el[1, x])
        iz_out[x] = iz
        h1 = mg[1, x]
        rhs = ds[x] * el[0, x] + ((iz - prev_y(iz, 0.0)) - (h1 - prev_z(h1))) * (1.0 / H)
        u = reduce_apply(rhs, 0, z_load(yk, x), yib[x])
        up_out[x] = u
        pair[0, x:x + 1] = u[0:1]
        pair[1, x:x + 1] = u[ny - 1:ny] - iz[ny - 1:ny] * (1.0 / H)


def chain_z_kernel(el, mg, ds, ex, h0_low, iy_out, up_out, pair):
    nx, ny, nz = ds.shape
    rhs = []
    below = jnp.zeros((ny, nz), F32)
    for x in range(nx):
        e0 = el[0, x]
        iy = mg[1, x] - H * (next_z(e0) - e0)
        iy_out[x] = iy
        h0 = mg[0, x]
        rhs.append(ds[x] * el[2, x] + ((iy - below) - (h0 - prev_y(h0, h0_low[x:x + 1]))) * (1.0 / H))
        below = iy
    sweep_x(rhs, ex, up_out)
    pair[0] = up_out[0]
    pair[1] = up_out[nx - 1] - below * (1.0 / H)


def center_y_kernel(el, mg, ds, zk, zib, e2_up, h2_low, sx_out, t1_out):
    nx, ny, nz = ds.shape
    for x in range(nx):
        e2 = el[2, x]
        ix = mg[0, x] - H * (next_y(e2, e2_up[x:x + 1]) - e2)
        below = mg[2, x - 1] if x > 0 else h2_low[0]
        rhs = ds[x] * el[1, x] + ((ix - prev_z(ix)) - (mg[2, x] - below)) * (1.0 / H)
        cy = reduce_apply(rhs, 1, z_load(zk, x), zib[x])
        curl = H * (next_z(cy) - cy)
        mx = ix + curl
        sx_out[x] = mx + curl
        t1_out[x] = ds[x] * cy + (mx - prev_z(mx)) * (1.0 / H)


def scan_y_kernel(ready, recv, own, pair, weights, consts, send, h0_low, e2_up, mixed):
    ky = lax.axis_index("gy")
    n = recv.shape[0]
    h0_low[...] = jnp.where(ky == 0, 0.0, recv[jnp.maximum(ky - 1, 0), 3])
    e2_up[...] = jnp.where(ky == n - 1, 0.0, recv[jnp.minimum(ky + 1, n - 1), 3])
    interface_factors(lambda j: (recv[j, 0], recv[j, 1], recv[j, 2]), (own[0], own[1], own[2]),
                      n, ky, weights, mixed, consts)
    ready()
    fill_send(send, pair[0], pair[1], consts, n, ky)


def half_x_kernel(nxd, ready, recv, weights, consts, pair_x, up, iz, t1, ds, phy, psy, ex, coef_x, pair_z, sz_out, t4_out, ufy_out, send, edge):
    ky = lax.axis_index("gy")
    nx, ny, nz = ds.shape
    A, C = gather_sums(recv, weights, recv.shape[0], ky)
    lower, upper = boundary(A, C, pair_x[0], pair_x[1], consts)
    edge[0] = lower
    edge[1] = upper
    ready()
    rhs = []
    below = jnp.zeros((ny, nz), F32)
    for x in range(nx):
        lo = edge[0, x:x + 1]
        hi = edge[1, x:x + 1]
        cx = up[x] + phy[x] * lo + psy[x] * hi
        curl = H * (next_y(cx, hi) - cx)
        mz = iz[x] + curl
        sz = mz + curl
        sz_out[x] = sz
        mlow = jnp.where(ky == 0, 0.0, H * (cx[0:1] - lo))
        t4_out[x] = ds[x] * cx + (mz - prev_y(mz, mlow)) * (1.0 / H)
        rhs.append(t1[x] - (sz - below) * (1.0 / H))
        below = sz
    sweep_x(rhs, ex, ufy_out)
    f = ufy_out[0]
    l = ufy_out[nx - 1] + below * (1.0 / H)
    for j in range(nxd):
        for i in range(3):
            send[j, i] = coef_x[i]
        send[j, 3] = pair_z[0]
        send[j, 4] = pair_z[1]
        send[j, 5] = f
        send[j, 6] = l


def half_z_kernel(ready, recv, cx, pair_z, up, iy, sx, ufy, sz, ds, phx, psx, yk, yib, consts_y, sy_out, ufz_out, pair_out, edge_y_out, send, weights, mixed, consts):
    kx = lax.axis_index("gx")
    ky = lax.axis_index("gy")
    nx, ny, nz = ds.shape
    n = recv.shape[0]
    interface_factors(lambda j: (recv[j, 0], recv[j, 1], recv[j, 2]), (cx[0], cx[1], cx[2]), n, kx, weights, mixed, consts)
    A, C = gather_sums_pair(lambda j: (recv[j, 5], recv[j, 6]), weights, mixed, n, kx)
    ready()
    lower, upper = boundary(A, C, ufy[0], ufy[nx - 1] + sz[nx - 1] * (1.0 / H), consts)
    edge_y_out[0] = lower
    edge_y_out[1] = upper
    A, C = gather_sums_pair(lambda j: (recv[j, 3], recv[j, 4]), weights, mixed, n, kx)
    lower, upper = boundary(A, C, pair_z[0], pair_z[1], consts)
    cz = up[0] + phx[0] * lower + psx[0] * upper
    below = jnp.where(kx == 0, 0.0, H * (cz - lower))
    for x in range(nx):
        cn = up[x + 1] + phx[x + 1] * lower + psx[x + 1] * upper if x < nx - 1 else upper
        curl = H * (cn - cz)
        my = iy[x] + curl
        sy_out[x] = my + curl
        s = sx[x]
        rhs = ds[x] * cz + ((my - below) - (s - prev_y(s, 0.0))) * (1.0 / H)
        u = reduce_apply(rhs, 0, z_load(yk, x), yib[x])
        ufz_out[x] = u
        pair_out[0, x:x + 1] = u[0:1]
        pair_out[1, x:x + 1] = u[ny - 1:ny] + s[ny - 1:ny] * (1.0 / H)
        cz = cn
        below = my
    fill_send(send, pair_out[0], pair_out[1], consts_y, send.shape[0], ky)


def final_x_kernel(t4, sy, zk, zib, fx_out, my_out):
    nx = t4.shape[0]
    for x in range(nx):
        s = sy[x]
        fx = reduce_apply(t4[x] - (s - prev_z(s)) * (1.0 / H), 1, z_load(zk, x), zib[x])
        fx_out[x] = fx
        my_out[x] = s - H * (next_z(fx) - fx)


def final_y_kernel(edge, up, sz, phx, psx, fy_out, mz_out):
    nx = up.shape[0]
    lower = edge[0]
    upper = edge[1]
    fy = up[0] + phx[0] * lower + psx[0] * upper
    for x in range(nx):
        fn = up[x + 1] + phx[x + 1] * lower + psx[x + 1] * upper if x < nx - 1 else upper
        fy_out[x] = fy
        mz_out[x] = sz[x] - H * (fn - fy)
        fy = fn


def final_z_kernel(ready, recv, weights, consts, pair, up, sx, phy, psy, fx, fy, my, mz, e_out, h_out, edge):
    ky = lax.axis_index("gy")
    nx = up.shape[0]
    A, C = gather_sums(recv, weights, recv.shape[0], ky)
    lower, upper = boundary(A, C, pair[0], pair[1], consts)
    ready()
    edge[0] = lower
    edge[1] = upper
    for x in range(nx):
        lo = edge[0, x:x + 1]
        hi = edge[1, x:x + 1]
        fz = up[x] + phy[x] * lo + psy[x] * hi
        e_out[0, x] = fx[x]
        e_out[1, x] = fy[x]
        e_out[2, x] = fz
        h_out[0, x] = sx[x] - H * (next_y(fz, hi) - fz)
        h_out[1, x] = my[x]
        h_out[2, x] = mz[x]


def staged(kernel, kinds_in, kinds_out, first):
    def body(*refs):
        ni = len(kinds_in)
        no = len(kinds_out)
        ins = refs[:ni]
        outs = refs[ni:ni + no]
        rest = list(refs[ni + no:])
        sems = rest.pop()
        work = []
        copies = []
        for ref, kind in zip(ins, kinds_in):
            if kind == "v":
                work.append(ref)
                continue
            held = rest.pop(0)
            copy = pltpu.make_async_copy(ref, held, sems.at[len(copies)])
            copy.start()
            copies.append(copy)
            work.append(held)
        back = []
        for ref, kind in zip(outs, kinds_out):
            if kind == "v":
                work.append(ref)
                continue
            held = rest.pop(0)
            back.append((held, ref))
            work.append(held)
        head = len(copies) if first is None else first
        for copy in copies[:head]:
            copy.wait()

        def ready():
            for copy in copies[head:]:
                copy.wait()

        if first is None:
            kernel(*work, *rest)
        else:
            kernel(ready, *work, *rest)
        copies = [pltpu.make_async_copy(held, ref, sems.at[i]) for i, (held, ref) in enumerate(back)]
        for copy in copies:
            copy.start()
        for copy in copies:
            copy.wait()

    return body


def call(kernel, outs, *args, smem=(), near=(), near_out=(), scratch=(), first=None, room=ROOM, name=None):
    kinds_in = ["s" if i in smem else "v" if i in near else "h" for i in range(len(args))]
    kinds_out = ["v" if i in near_out else "h" for i in range(len(outs))]
    held = []
    for a, kind in zip(args, kinds_in):
        if kind != "v":
            held.append((pltpu.SMEM if kind == "s" else pltpu.VMEM)(a.shape, a.dtype))
    for o, kind in zip(outs, kinds_out):
        if kind != "v":
            held.append(pltpu.VMEM(o, F32))
    spec = {"v": pltpu.VMEM, "h": HBM, "s": HBM}
    nbytes = sum(4 * _size(a.shape) for a in args) + sum(4 * _size(o) for o in outs)
    return pl.pallas_call(
        staged(kernel, kinds_in, kinds_out, first),
        out_shape=[jax.ShapeDtypeStruct(o, F32) for o in outs],
        in_specs=[pl.BlockSpec(memory_space=spec[k]) for k in kinds_in],
        out_specs=[pl.BlockSpec(memory_space=spec[k]) for k in kinds_out],
        scratch_shapes=held + list(scratch) + [pltpu.SemaphoreType.DMA((len(held),))],
        cost_estimate=pl.CostEstimate(flops=4 * nbytes, bytes_accessed=nbytes, transcendentals=0),
        compiler_params=pltpu.CompilerParams(vmem_limit_bytes=room << 20),
        name=name,
    )(*args)


def _size(shape):
    n = 1
    for d in shape:
        n *= d
    return n


def shifted(array, axis, by):
    count = lax.axis_size(axis)
    return lax.ppermute(array, axis, [(i, i + by) for i in range(count) if 0 <= i + by < count])


def exchange(array, axis):
    return lax.all_to_all(array, axis, 0, 0)


def per_device(electric, magnetic, material, permittivity, conductivity):
    nxd = lax.axis_size("gx")
    nyd = lax.axis_size("gy")
    cell = material.shape
    nx, ny, nz = cell
    py = (nx, nz)
    px = (ny, nz)

    def bind(kernel, *lead):
        def body(*refs):
            kernel(*lead, *refs)
        return body


    ds, si, yk, yib, phy, psy, cy, send_c, pe1, ph2 = call(
        bind(coef_kernel, nyd),
        [cell, cell, (2 * len(strides(ny)),) + cell, cell, cell, cell, (3,) + py, (nyd, 4) + py,
         (1,) + px, (1,) + px],
        material, permittivity, conductivity, electric, magnetic, smem=(1, 2), first=3, room=60,
        scratch=[pltpu.VMEM(py, F32), pltpu.VMEM(py, F32)], name="coef")
    recv_c = exchange(send_c, "gy")
    e1_up = shifted(pe1, "gx", -1)
    h2_low = shifted(ph2, "gx", 1)
    zk, zib, ex, phx, psx, cx = call(
        bind(factor_kernel, nxd), [(2 * len(strides(nz)),) + cell, cell, cell, cell, cell, (3,) + px], si, name="factor")
    e1_up, h2_low, cx = lax.optimization_barrier((e1_up, h2_low, cx))
    iz, ux, pair_x = call(chain_x_kernel, [cell, cell, (2,) + py],
                          electric, magnetic, ds, yk, yib, e1_up, name="chain_x")
    wy, ky, send1, h0_low, e2_up = call(scan_y_kernel, [(nyd,) + py, (9,) + py, (nyd,) + py, py, py], recv_c, cy, pair_x,
                         first=2, scratch=[pltpu.VMEM((nyd,) + py, F32)], name="scan_y")
    recv1 = exchange(send1, "gy")

    iy, uz, pair_z = call(chain_z_kernel, [cell, cell, (2,) + px], electric, magnetic, ds, ex, h0_low, name="chain_z")
    sx, t1 = call(center_y_kernel, [cell, cell], electric, magnetic, ds, zk, zib, e2_up, h2_low, name="center_y")

    sz, t4, ufy, send2 = call(
        bind(half_x_kernel, nxd), [cell, cell, cell, (nxd, 7) + px],
        recv1, wy, ky, pair_x, ux, iz, t1, ds, phy, psy, ex, cx, pair_z,
        first=4, scratch=[pltpu.VMEM((2,) + py, F32)], name="half_x")
    recv2 = exchange(send2, "gx")
    sy, ufz, pair4, edge_y, send3 = call(
        half_z_kernel, [cell, cell, (2,) + py, (2,) + px, (nyd,) + py],
        recv2, cx, pair_z, uz, iy, sx, ufy, sz, ds, phx, psx, yk, yib, ky,
        first=2, scratch=[pltpu.VMEM((nxd,) + px, F32), pltpu.VMEM((nxd,) + px, F32), pltpu.VMEM((9,) + px, F32)],
        name="half_z")
    recv3 = exchange(send3, "gy")
    fx, my = call(final_x_kernel, [cell, cell], t4, sy, zk, zib, name="final_x")
    fy, mz = call(final_y_kernel, [cell, cell], edge_y, ufy, sz, phx, psx, name="final_y")
    e, h = call(final_z_kernel, [(3,) + cell, (3,) + cell],
                recv3, wy, ky, pair4, ufz, sx, phy, psy, fx, fy, my, mz,
                first=4, scratch=[pltpu.VMEM((2,) + py, F32)], name="final_z")
    return e, h


def solution(mesh):
    return jax.shard_map(
        per_device,
        mesh=mesh,
        in_specs=(
            P(None, "gx", "gy", None),
            P(None, "gx", "gy", None),
            P("gx", "gy", None),
            P(),
            P(),
        ),
        out_specs=(P(None, "gx", "gy", None), P(None, "gx", "gy", None)),
        check_vma=False,
    )
```

```python
import jax
import jax.numpy as jnp
from jax import lax
from jax.experimental import pallas as pl
from jax.experimental.pallas import tpu as pltpu
from jax.sharding import PartitionSpec as P

H = 12.0
F32 = jnp.float32
HBM = pltpu.HBM
ROOM = 60


def iota(axis, shape):
    return lax.broadcasted_iota(jnp.int32, shape, axis)


def next_z(v):
    n = v.shape[1]
    return jnp.where(iota(1, v.shape) == n - 1, 0.0, pltpu.roll(v, n - 1, 1))


def prev_z(v):
    return jnp.where(iota(1, v.shape) == 0, 0.0, pltpu.roll(v, 1, 1))


def next_y(v, row):
    n = v.shape[0]
    return jnp.where(iota(0, v.shape) == n - 1, row, pltpu.roll(v, n - 1, 0))


def prev_y(v, row):
    return jnp.where(iota(0, v.shape) == 0, row, pltpu.roll(v, 1, 0))


def strides(n):
    out = []
    s = 1
    while s < n:
        out.append(s)
        s *= 2
    return out


def reduce_factors(a, b, axis, store):
    n = a.shape[axis]
    for level, s in enumerate(strides(n)):
        inv = 1.0 / b
        c = pltpu.roll(a, n - s, axis)
        ka = -a * pltpu.roll(inv, s, axis)
        kc = -c * pltpu.roll(inv, n - s, axis)
        store(level, ka, kc)
        b = b + ka * a + kc * c
        a = ka * pltpu.roll(a, s, axis)
    return 1.0 / b


def reduce_apply(r, axis, load, inv):
    n = r.shape[axis]
    for level, s in enumerate(strides(n)):
        ka, kc = load(level)
        r = r + ka * pltpu.roll(r, s, axis) + kc * pltpu.roll(r, n - s, axis)
    return r * inv


def sweep_x(rhs, ex, out):
    nx = len(rhs)
    fwd = [rhs[0]]
    for i in range(1, nx):
        fwd.append(rhs[i] + ex[i - 1] * fwd[i - 1])
    u = ex[nx - 1] * fwd[nx - 1]
    out[nx - 1] = u
    for i in range(nx - 2, -1, -1):
        u = ex[i] * (fwd[i] + u)
        out[i] = u


def interface_factors(coef, own, n, k, weights, mixed, consts):
    zero = jnp.zeros_like(own[0])
    B = zero
    for j in range(n - 1):
        al, be, de = coef(j)
        g = be / (1.0 - al * B)
        h = g * B
        weights[j] = g
        mixed[j] = h
        B = jnp.where(j < k, de + h * be, B)
    D = zero
    for j in range(n - 1, 0, -1):
        al, be, de = coef(j)
        g = be / (1.0 - de * D)
        h = g * D
        weights[j] = jnp.where(j > k, g, weights[j]) if j < n - 1 else g
        mixed[j] = jnp.where(j > k, h, mixed[j]) if j < n - 1 else h
        D = jnp.where(j > k, al + h * be, D)
    al, be, de = own
    den = 1.0 / (1.0 - al * B)
    gl = be * den
    bp = de + gl * be * B
    consts[0] = gl * B
    consts[1] = be * D / (1.0 - de * D)
    consts[2] = gl
    consts[3] = bp
    consts[4] = 1.0 / (1.0 - bp * D)
    consts[5] = D
    consts[6] = den
    consts[7] = den * al
    consts[8] = B


def to_right(f, l, consts):
    return l + consts[0] * f


def to_left(f, l, consts):
    return f + consts[1] * l


def boundary(A, C, f, l, consts):
    v = (to_right(f, l, consts) + consts[2] * A + consts[3] * C) * consts[4]
    upper = C + consts[5] * v
    first = consts[6] * f + consts[7] * A + consts[2] * upper
    lower = A + consts[8] * first
    return lower, upper


def gather_sums(recv, weights, n, k):
    A = jnp.zeros_like(recv[0])
    for j in range(n - 1):
        A = jnp.where(j < k, recv[j] + weights[j] * A, A)
    C = jnp.zeros_like(A)
    for j in range(n - 1, 0, -1):
        C = jnp.where(j > k, recv[j] + weights[j] * C, C)
    return A, C


def gather_sums_pair(pair, weights, mixed, n, k):
    A = jnp.zeros_like(weights[0])
    for j in range(n - 1):
        f, l = pair(j)
        A = jnp.where(j < k, l + mixed[j] * f + weights[j] * A, A)
    C = jnp.zeros_like(A)
    for j in range(n - 1, 0, -1):
        f, l = pair(j)
        C = jnp.where(j > k, f + mixed[j] * l + weights[j] * C, C)
    return A, C


def fill_send(send, f, l, consts, n, k):
    right = to_right(f, l, consts)
    left = to_left(f, l, consts)
    for j in range(n):
        send[j] = jnp.where(j > k, right, left)


def coef_kernel(nyd, ready, mat, perm, cond, el, mg, ds, si, yk, yib, phy, psy, cy, send, pe1, ph2, pe2, ph0):
    ky = lax.axis_index("gy")
    nx, ny, nz = mat.shape
    row = iota(0, (ny, nz))
    for x in range(nx):
        m = mat[x]
        eps = jnp.full(m.shape, perm[0], F32)
        sig = jnp.full(m.shape, cond[0], F32)
        for t in range(1, perm.shape[0]):
            eps = jnp.where(m == t, perm[t], eps)
            sig = jnp.where(m == t, cond[t], sig)
        ea = eps * (1.0 / (H * H))
        sh = sig * (0.5 / H)
        ds[x] = ea - sh
        inv_s = ea + sh
        si[x] = inv_s
        first = row == 0
        last = row == ny - 1
        a = jnp.where(first, 0.0, jnp.full(m.shape, -1.0, F32))
        b = inv_s + jnp.where(first, jnp.where(ky == 0, 1.0, 2.0), 2.0)

        def store(level, ka, kc):
            yk[2 * level, x] = ka
            yk[2 * level + 1, x] = kc

        def load(level):
            return yk[2 * level, x], yk[2 * level + 1, x]

        ib = reduce_factors(a, b, 0, store)
        yib[x] = ib
        lo = reduce_apply(jnp.where(first, jnp.where(ky == 0, 0.0, 1.0), jnp.zeros(m.shape, F32)), 0, load, ib)
        up = reduce_apply(jnp.where(last, jnp.where(ky == nyd - 1, 0.0, 1.0), jnp.zeros(m.shape, F32)), 0, load, ib)
        phy[x] = lo
        psy[x] = up
        cy[0, x:x + 1] = lo[0:1]
        cy[1, x:x + 1] = up[0:1]
        cy[2, x:x + 1] = up[ny - 1:ny]
    for j in range(nyd):
        send[j, 0:3] = cy[...]
    ready()
    pe1[0] = el[1, 0]
    ph2[0] = mg[2, nx - 1]
    for x in range(nx):
        pe2[x:x + 1] = el[2, x][0:1]
        ph0[x:x + 1] = mg[0, x][ny - 1:ny]
    for j in range(nyd):
        send[j, 3] = jnp.where(j > ky, ph0[...], pe2[...])


def z_solve(si, rhs):
    n = rhs.shape[1]
    lane = iota(1, rhs.shape)
    a = jnp.where(lane == 0, 0.0, jnp.full(rhs.shape, -1.0, F32))
    b = si + jnp.where(lane == 0, 1.0, jnp.full(rhs.shape, 2.0, F32))
    r = rhs
    for s in strides(n):
        inv = 1.0 / b
        c = pltpu.roll(a, n - s, 1)
        ka = -a * pltpu.roll(inv, s, 1)
        kc = -c * pltpu.roll(inv, n - s, 1)
        r = r + ka * pltpu.roll(r, s, 1) + kc * pltpu.roll(r, n - s, 1)
        b = b + ka * a + kc * c
        a = ka * pltpu.roll(a, s, 1)
    return r / b


def factor_kernel(nxd, si, zk, zib, ex, phx, psx, cx):
    kx = lax.axis_index("gx")
    nx, ny, nz = si.shape
    lane = iota(1, (ny, nz))
    for x in range(nx):
        a = jnp.where(lane == 0, 0.0, jnp.full((ny, nz), -1.0, F32))
        b = si[x] + jnp.where(lane == 0, 1.0, jnp.full((ny, nz), 2.0, F32))

        def store(level, ka, kc):
            zk[2 * level, x] = ka
            zk[2 * level + 1, x] = kc

        zib[x] = reduce_factors(a, b, 1, store)
    d = si[0] + jnp.where(kx == 0, 1.0, 2.0)
    r = jnp.full((ny, nz), jnp.where(kx == 0, 0.0, 1.0), F32)
    phx[0] = r
    for x in range(nx):
        e = 1.0 / d
        ex[x] = e
        if x < nx - 1:
            d = si[x + 1] + (2.0 - e)
            r = e * r
            phx[x + 1] = r
    u = ex[nx - 1] * r
    w = ex[nx - 1] * jnp.where(kx == nxd - 1, 0.0, 1.0)
    phx[nx - 1] = u
    psx[nx - 1] = w
    cx[2] = w
    for x in range(nx - 2, -1, -1):
        u = ex[x] * (phx[x] + u)
        w = ex[x] * w
        phx[x] = u
        psx[x] = w
    cx[0] = u
    cx[1] = w


def z_load(zk, x):
    return lambda level: (zk[2 * level, x], zk[2 * level + 1, x])


def chain_x_kernel(el, mg, ds, yk, yib, e1_up, iz_out, up_out, pair):
    nx, ny, nz = ds.shape
    for x in range(nx):
        above = el[1, x + 1] if x < nx - 1 else e1_up[0]
        iz = mg[2, x] - H * (above - el[1, x])
        iz_out[x] = iz
        h1 = mg[1, x]
        rhs = ds[x] * el[0, x] + ((iz - prev_y(iz, 0.0)) - (h1 - prev_z(h1))) * (1.0 / H)
        u = reduce_apply(rhs, 0, z_load(yk, x), yib[x])
        up_out[x] = u
        pair[0, x:x + 1] = u[0:1]
        pair[1, x:x + 1] = u[ny - 1:ny] - iz[ny - 1:ny] * (1.0 / H)


def chain_z_kernel(el, mg, ds, ex, halo_y, iy_out, up_out, pair):
    nx, ny, nz = ds.shape
    rhs = []
    below = jnp.zeros((ny, nz), F32)
    for x in range(nx):
        e0 = el[0, x]
        iy = mg[1, x] - H * (next_z(e0) - e0)
        iy_out[x] = iy
        h0 = mg[0, x]
        rhs.append(ds[x] * el[2, x] + ((iy - below) - (h0 - prev_y(h0, halo_y[0, x:x + 1]))) * (1.0 / H))
        below = iy
    sweep_x(rhs, ex, up_out)
    pair[0] = up_out[0]
    pair[1] = up_out[nx - 1] - below * (1.0 / H)


def center_y_kernel(el, mg, ds, zk, zib, halo_y, h2_low, sx_out, t1_out):
    nx, ny, nz = ds.shape
    for x in range(nx):
        e2 = el[2, x]
        ix = mg[0, x] - H * (next_y(e2, halo_y[1, x:x + 1]) - e2)
        below = mg[2, x - 1] if x > 0 else h2_low[0]
        rhs = ds[x] * el[1, x] + ((ix - prev_z(ix)) - (mg[2, x] - below)) * (1.0 / H)
        cy = reduce_apply(rhs, 1, z_load(zk, x), zib[x])
        curl = H * (next_z(cy) - cy)
        mx = ix + curl
        sx_out[x] = mx + curl
        t1_out[x] = ds[x] * cy + (mx - prev_z(mx)) * (1.0 / H)


def scan_y_kernel(ready, recv, own, pair, weights, consts, send, halo, mixed):
    ky = lax.axis_index("gy")
    n = recv.shape[0]
    halo[0] = jnp.where(ky == 0, 0.0, recv[jnp.maximum(ky - 1, 0), 3])
    halo[1] = jnp.where(ky == n - 1, 0.0, recv[jnp.minimum(ky + 1, n - 1), 3])
    interface_factors(lambda j: (recv[j, 0], recv[j, 1], recv[j, 2]), (own[0], own[1], own[2]),
                      n, ky, weights, mixed, consts)
    ready()
    fill_send(send, pair[0], pair[1], consts, n, ky)


def half_x_kernel(nxd, ready, recv, weights, consts, pair_x, up, iz, t1, ds, phy, psy, ex, coef_x, pair_z, sz_out, t4_out, ufy_out, send, edge):
    ky = lax.axis_index("gy")
    nx, ny, nz = ds.shape
    A, C = gather_sums(recv, weights, recv.shape[0], ky)
    lower, upper = boundary(A, C, pair_x[0], pair_x[1], consts)
    edge[0] = lower
    edge[1] = upper
    ready()
    rhs = []
    below = jnp.zeros((ny, nz), F32)
    for x in range(nx):
        lo = edge[0, x:x + 1]
        hi = edge[1, x:x + 1]
        cx = up[x] + phy[x] * lo + psy[x] * hi
        curl = H * (next_y(cx, hi) - cx)
        mz = iz[x] + curl
        sz = mz + curl
        sz_out[x] = sz
        mlow = jnp.where(ky == 0, 0.0, H * (cx[0:1] - lo))
        t4_out[x] = ds[x] * cx + (mz - prev_y(mz, mlow)) * (1.0 / H)
        rhs.append(t1[x] - (sz - below) * (1.0 / H))
        below = sz
    sweep_x(rhs, ex, ufy_out)
    f = ufy_out[0]
    l = ufy_out[nx - 1] + below * (1.0 / H)
    for j in range(nxd):
        for i in range(3):
            send[j, i] = coef_x[i]
        send[j, 3] = pair_z[0]
        send[j, 4] = pair_z[1]
        send[j, 5] = f
        send[j, 6] = l


def half_z_kernel(ready, recv, cx, pair_z, up, iy, sx, ufy, sz, ds, phx, psx, yk, yib, consts_y, sy_out, ufz_out, pair_out, edge_y_out, send, weights, mixed, consts):
    kx = lax.axis_index("gx")
    ky = lax.axis_index("gy")
    nx, ny, nz = ds.shape
    n = recv.shape[0]
    interface_factors(lambda j: (recv[j, 0], recv[j, 1], recv[j, 2]), (cx[0], cx[1], cx[2]), n, kx, weights, mixed, consts)
    A, C = gather_sums_pair(lambda j: (recv[j, 5], recv[j, 6]), weights, mixed, n, kx)
    ready()
    lower, upper = boundary(A, C, ufy[0], ufy[nx - 1] + sz[nx - 1] * (1.0 / H), consts)
    edge_y_out[0] = lower
    edge_y_out[1] = upper
    A, C = gather_sums_pair(lambda j: (recv[j, 3], recv[j, 4]), weights, mixed, n, kx)
    lower, upper = boundary(A, C, pair_z[0], pair_z[1], consts)
    cz = up[0] + phx[0] * lower + psx[0] * upper
    below = jnp.where(kx == 0, 0.0, H * (cz - lower))
    for x in range(nx):
        cn = up[x + 1] + phx[x + 1] * lower + psx[x + 1] * upper if x < nx - 1 else upper
        curl = H * (cn - cz)
        my = iy[x] + curl
        sy_out[x] = my + curl
        s = sx[x]
        rhs = ds[x] * cz + ((my - below) - (s - prev_y(s, 0.0))) * (1.0 / H)
        u = reduce_apply(rhs, 0, z_load(yk, x), yib[x])
        ufz_out[x] = u
        pair_out[0, x:x + 1] = u[0:1]
        pair_out[1, x:x + 1] = u[ny - 1:ny] + s[ny - 1:ny] * (1.0 / H)
        cz = cn
        below = my
    fill_send(send, pair_out[0], pair_out[1], consts_y, send.shape[0], ky)


def final_x_kernel(t4, sy, si, fx_out, my_out):
    nx = t4.shape[0]
    for x in range(nx):
        s = sy[x]
        fx = z_solve(si[x], t4[x] - (s - prev_z(s)) * (1.0 / H))
        fx_out[x] = fx
        my_out[x] = s - H * (next_z(fx) - fx)


def final_y_kernel(edge, up, sz, phx, psx, fy_out, mz_out):
    nx = up.shape[0]
    lower = edge[0]
    upper = edge[1]
    fy = up[0] + phx[0] * lower + psx[0] * upper
    for x in range(nx):
        fn = up[x + 1] + phx[x + 1] * lower + psx[x + 1] * upper if x < nx - 1 else upper
        fy_out[x] = fy
        mz_out[x] = sz[x] - H * (fn - fy)
        fy = fn


def final_z_kernel(ready, recv, weights, consts, pair, up, sx, phy, psy, fx, fy, my, mz, e_out, h_out, edge):
    ky = lax.axis_index("gy")
    nx = up.shape[0]
    A, C = gather_sums(recv, weights, recv.shape[0], ky)
    lower, upper = boundary(A, C, pair[0], pair[1], consts)
    ready()
    edge[0] = lower
    edge[1] = upper
    for x in range(nx):
        lo = edge[0, x:x + 1]
        hi = edge[1, x:x + 1]
        fz = up[x] + phy[x] * lo + psy[x] * hi
        e_out[0, x] = fx[x]
        e_out[1, x] = fy[x]
        e_out[2, x] = fz
        h_out[0, x] = sx[x] - H * (next_y(fz, hi) - fz)
        h_out[1, x] = my[x]
        h_out[2, x] = mz[x]


def staged(kernel, kinds_in, kinds_out, first):
    def body(*refs):
        ni = len(kinds_in)
        no = len(kinds_out)
        ins = refs[:ni]
        outs = refs[ni:ni + no]
        rest = list(refs[ni + no:])
        sems = rest.pop()
        work = []
        copies = []
        for ref, kind in zip(ins, kinds_in):
            if kind == "v":
                work.append(ref)
                continue
            held = rest.pop(0)
            copy = pltpu.make_async_copy(ref, held, sems.at[len(copies)])
            copy.start()
            copies.append(copy)
            work.append(held)
        back = []
        for ref, kind in zip(outs, kinds_out):
            if kind == "v":
                work.append(ref)
                continue
            held = rest.pop(0)
            back.append((held, ref))
            work.append(held)
        head = len(copies) if first is None else first
        for copy in copies[:head]:
            copy.wait()

        def ready():
            for copy in copies[head:]:
                copy.wait()

        if first is None:
            kernel(*work, *rest)
        else:
            kernel(ready, *work, *rest)
        copies = [pltpu.make_async_copy(held, ref, sems.at[i]) for i, (held, ref) in enumerate(back)]
        for copy in copies:
            copy.start()
        for copy in copies:
            copy.wait()

    return body


def call(kernel, outs, *args, smem=(), near=(), near_out=(), scratch=(), first=None, room=ROOM, hot=False, far=(), name=None):
    kinds_in = ["s" if i in smem else "v" if i in near or (hot and i not in far) else "h" for i in range(len(args))]
    kinds_out = ["v" if i in near_out or (hot and name.startswith(("final_x", "final_y"))) else "h" for i in range(len(outs))]
    held = []
    for a, kind in zip(args, kinds_in):
        if kind != "v":
            held.append((pltpu.SMEM if kind == "s" else pltpu.VMEM)(a.shape, a.dtype))
    for o, kind in zip(outs, kinds_out):
        if kind != "v":
            held.append(pltpu.VMEM(o, F32))
    spec = {"v": pltpu.VMEM, "h": HBM, "s": HBM}
    nbytes = sum(4 * _size(a.shape) for a in args) + sum(4 * _size(o) for o in outs)
    return pl.pallas_call(
        staged(kernel, kinds_in, kinds_out, 0 if hot and first is not None else first),
        out_shape=[jax.ShapeDtypeStruct(o, F32) for o in outs],
        in_specs=[pl.BlockSpec(memory_space=spec[k]) for k in kinds_in],
        out_specs=[pl.BlockSpec(memory_space=spec[k]) for k in kinds_out],
        scratch_shapes=held + list(scratch) + [pltpu.SemaphoreType.DMA((max(len(held), 1),))],
        cost_estimate=pl.CostEstimate(flops=4 * nbytes, bytes_accessed=nbytes, transcendentals=0),
        compiler_params=pltpu.CompilerParams(vmem_limit_bytes=room << 20),
        name=name,
    )(*args)


def _size(shape):
    n = 1
    for d in shape:
        n *= d
    return n


def shifted(array, axis, by):
    count = lax.axis_size(axis)
    return lax.ppermute(array, axis, [(i, i + by) for i in range(count) if 0 <= i + by < count])


def exchange(array, axis):
    return lax.all_to_all(array, axis, 0, 0)


def per_device(electric, magnetic, material, permittivity, conductivity):
    nxd = lax.axis_size("gx")
    nyd = lax.axis_size("gy")
    cell = material.shape
    nx, ny, nz = cell
    py = (nx, nz)
    px = (ny, nz)

    def bind(kernel, *lead):
        def body(*refs):
            kernel(*lead, *refs)
        return body


    ds, si, yk, yib, phy, psy, cy, send_c, pe1, ph2 = call(
        bind(coef_kernel, nyd),
        [cell, cell, (2 * len(strides(ny)),) + cell, cell, cell, cell, (3,) + py, (nyd, 4) + py,
         (1,) + px, (1,) + px],
        material, permittivity, conductivity, electric, magnetic, smem=(1, 2), first=3, room=60,
        scratch=[pltpu.VMEM(py, F32), pltpu.VMEM(py, F32)], name="coef")
    recv_c = exchange(send_c, "gy")
    e1_up = shifted(pe1, "gx", -1)
    h2_low = shifted(ph2, "gx", 1)
    zk, zib, ex, phx, psx, cx = call(
        bind(factor_kernel, nxd), [(2 * len(strides(nz)),) + cell, cell, cell, cell, cell, (3,) + px], si, name="factor")
    e1_up, h2_low, cx = lax.optimization_barrier((e1_up, h2_low, cx))
    iz, ux, pair_x = call(chain_x_kernel, [cell, cell, (2,) + py],
                          electric, magnetic, ds, yk, yib, e1_up, hot=True, far=(0, 1), room=40, name="chain_x")
    wy, ky, send1, halo_y = call(scan_y_kernel, [(nyd,) + py, (9,) + py, (nyd,) + py, (2,) + py], recv_c, cy, pair_x,
                         first=2, scratch=[pltpu.VMEM((nyd,) + py, F32)], hot=True, room=40, name="scan_y")
    recv1 = exchange(send1, "gy")

    iy, uz, pair_z = call(chain_z_kernel, [cell, cell, (2,) + px], electric, magnetic, ds, ex, halo_y, name="chain_z")
    sx, t1 = call(center_y_kernel, [cell, cell], electric, magnetic, ds, zk, zib, halo_y, h2_low, name="center_y")

    sz, t4, ufy, send2 = call(
        bind(half_x_kernel, nxd), [cell, cell, cell, (nxd, 7) + px],
        recv1, wy, ky, pair_x, ux, iz, t1, ds, phy, psy, ex, cx, pair_z,
        first=4, scratch=[pltpu.VMEM((2,) + py, F32)], hot=True, room=40, name="half_x")
    recv2 = exchange(send2, "gx")
    sy, ufz, pair4, edge_y, send3 = call(
        half_z_kernel, [cell, cell, (2,) + py, (2,) + px, (nyd,) + py],
        recv2, cx, pair_z, uz, iy, sx, ufy, sz, ds, phx, psx, yk, yib, ky,
        first=2, scratch=[pltpu.VMEM((nxd,) + px, F32), pltpu.VMEM((nxd,) + px, F32), pltpu.VMEM((9,) + px, F32)],
        hot=True, room=40, name="half_z")
    recv3 = exchange(send3, "gy")
    fx, my = call(final_x_kernel, [cell, cell], t4, sy, si, hot=True, room=40, name="final_x")
    fy, mz = call(final_y_kernel, [cell, cell], edge_y, ufy, sz, phx, psx, hot=True, room=40, name="final_y")
    e, h = call(final_z_kernel, [(3,) + cell, (3,) + cell],
                recv3, wy, ky, pair4, ufz, sx, phy, psy, fx, fy, my, mz,
                first=4, scratch=[pltpu.VMEM((2,) + py, F32)], hot=True, room=40, name="final_z")
    return e, h


def solution(mesh):
    return jax.shard_map(
        per_device,
        mesh=mesh,
        in_specs=(
            P(None, "gx", "gy", None),
            P(None, "gx", "gy", None),
            P("gx", "gy", None),
            P(),
            P(),
        ),
        out_specs=(P(None, "gx", "gy", None), P(None, "gx", "gy", None)),
        check_vma=False,
    )
```

```python
import jax
import jax.numpy as jnp
from jax import lax
from jax.experimental import pallas as pl
from jax.experimental.pallas import tpu as pltpu
from jax.sharding import PartitionSpec as P

H = 12.0
F32 = jnp.float32
HBM = pltpu.HBM
ROOM = 60


def iota(axis, shape):
    return lax.broadcasted_iota(jnp.int32, shape, axis)


def next_z(v):
    n = v.shape[1]
    return jnp.where(iota(1, v.shape) == n - 1, 0.0, pltpu.roll(v, n - 1, 1))


def prev_z(v):
    return jnp.where(iota(1, v.shape) == 0, 0.0, pltpu.roll(v, 1, 1))


def next_y(v, row):
    n = v.shape[0]
    return jnp.where(iota(0, v.shape) == n - 1, row, pltpu.roll(v, n - 1, 0))


def prev_y(v, row):
    return jnp.where(iota(0, v.shape) == 0, row, pltpu.roll(v, 1, 0))


def strides(n):
    out = []
    s = 1
    while s < n:
        out.append(s)
        s *= 2
    return out


def reduce_factors(a, b, axis, store):
    n = a.shape[axis]
    for level, s in enumerate(strides(n)):
        inv = 1.0 / b
        c = pltpu.roll(a, n - s, axis)
        ka = -a * pltpu.roll(inv, s, axis)
        kc = -c * pltpu.roll(inv, n - s, axis)
        store(level, ka, kc)
        b = b + ka * a + kc * c
        a = ka * pltpu.roll(a, s, axis)
    return 1.0 / b


def reduce_apply(r, axis, load, inv):
    n = r.shape[axis]
    for level, s in enumerate(strides(n)):
        ka, kc = load(level)
        r = r + ka * pltpu.roll(r, s, axis) + kc * pltpu.roll(r, n - s, axis)
    return r * inv


def sweep_x(rhs, ex, out):
    nx = len(rhs)
    fwd = [rhs[0]]
    for i in range(1, nx):
        fwd.append(rhs[i] + ex[i - 1] * fwd[i - 1])
    u = ex[nx - 1] * fwd[nx - 1]
    out[nx - 1] = u
    for i in range(nx - 2, -1, -1):
        u = ex[i] * (fwd[i] + u)
        out[i] = u


def interface_factors(coef, own, n, k, weights, mixed, consts):
    zero = jnp.zeros_like(own[0])
    B = zero
    for j in range(n - 1):
        al, be, de = coef(j)
        g = be / (1.0 - al * B)
        h = g * B
        weights[j] = g
        mixed[j] = h
        B = jnp.where(j < k, de + h * be, B)
    D = zero
    for j in range(n - 1, 0, -1):
        al, be, de = coef(j)
        g = be / (1.0 - de * D)
        h = g * D
        weights[j] = jnp.where(j > k, g, weights[j]) if j < n - 1 else g
        mixed[j] = jnp.where(j > k, h, mixed[j]) if j < n - 1 else h
        D = jnp.where(j > k, al + h * be, D)
    al, be, de = own
    den = 1.0 / (1.0 - al * B)
    gl = be * den
    bp = de + gl * be * B
    consts[0] = gl * B
    consts[1] = be * D / (1.0 - de * D)
    consts[2] = gl
    consts[3] = bp
    consts[4] = 1.0 / (1.0 - bp * D)
    consts[5] = D
    consts[6] = den
    consts[7] = den * al
    consts[8] = B


def to_right(f, l, consts):
    return l + consts[0] * f


def to_left(f, l, consts):
    return f + consts[1] * l


def boundary(A, C, f, l, consts):
    v = (to_right(f, l, consts) + consts[2] * A + consts[3] * C) * consts[4]
    upper = C + consts[5] * v
    first = consts[6] * f + consts[7] * A + consts[2] * upper
    lower = A + consts[8] * first
    return lower, upper


def gather_sums(recv, weights, n, k):
    A = jnp.zeros_like(recv[0])
    for j in range(n - 1):
        A = jnp.where(j < k, recv[j] + weights[j] * A, A)
    C = jnp.zeros_like(A)
    for j in range(n - 1, 0, -1):
        C = jnp.where(j > k, recv[j] + weights[j] * C, C)
    return A, C


def gather_sums_pair(pair, weights, mixed, n, k):
    A = jnp.zeros_like(weights[0])
    for j in range(n - 1):
        f, l = pair(j)
        A = jnp.where(j < k, l + mixed[j] * f + weights[j] * A, A)
    C = jnp.zeros_like(A)
    for j in range(n - 1, 0, -1):
        f, l = pair(j)
        C = jnp.where(j > k, f + mixed[j] * l + weights[j] * C, C)
    return A, C


def fill_send(send, f, l, consts, n, k):
    right = to_right(f, l, consts)
    left = to_left(f, l, consts)
    for j in range(n):
        send[j] = jnp.where(j > k, right, left)


def coef_kernel(nyd, ready, mat, perm, cond, el, mg, ds, si, yk, yib, phy, psy, cy, send, pe1, ph2, pe2, ph0):
    ky = lax.axis_index("gy")
    nx, ny, nz = mat.shape
    row = iota(0, (ny, nz))
    for x in range(nx):
        m = mat[x]
        eps = jnp.full(m.shape, perm[0], F32)
        sig = jnp.full(m.shape, cond[0], F32)
        for t in range(1, perm.shape[0]):
            eps = jnp.where(m == t, perm[t], eps)
            sig = jnp.where(m == t, cond[t], sig)
        ea = eps * (1.0 / (H * H))
        sh = sig * (0.5 / H)
        ds[x] = ea - sh
        inv_s = ea + sh
        si[x] = inv_s
        first = row == 0
        last = row == ny - 1
        a = jnp.where(first, 0.0, jnp.full(m.shape, -1.0, F32))
        b = inv_s + jnp.where(first, jnp.where(ky == 0, 1.0, 2.0), 2.0)

        def store(level, ka, kc):
            yk[2 * level, x] = ka
            yk[2 * level + 1, x] = kc

        def load(level):
            return yk[2 * level, x], yk[2 * level + 1, x]

        ib = reduce_factors(a, b, 0, store)
        yib[x] = ib
        lo = reduce_apply(jnp.where(first, jnp.where(ky == 0, 0.0, 1.0), jnp.zeros(m.shape, F32)), 0, load, ib)
        up = reduce_apply(jnp.where(last, jnp.where(ky == nyd - 1, 0.0, 1.0), jnp.zeros(m.shape, F32)), 0, load, ib)
        phy[x] = lo
        psy[x] = up
        cy[0, x:x + 1] = lo[0:1]
        cy[1, x:x + 1] = up[0:1]
        cy[2, x:x + 1] = up[ny - 1:ny]
    for j in range(nyd):
        send[j, 0:3] = cy[...]
    ready()
    pe1[0] = el[1, 0]
    ph2[0] = mg[2, nx - 1]
    for x in range(nx):
        pe2[x:x + 1] = el[2, x][0:1]
        ph0[x:x + 1] = mg[0, x][ny - 1:ny]
    for j in range(nyd):
        send[j, 3] = jnp.where(j > ky, ph0[...], pe2[...])


def z_solve(si, rhs):
    n = rhs.shape[1]
    lane = iota(1, rhs.shape)
    a = jnp.where(lane == 0, 0.0, jnp.full(rhs.shape, -1.0, F32))
    b = si + jnp.where(lane == 0, 1.0, jnp.full(rhs.shape, 2.0, F32))
    r = rhs
    for s in strides(n):
        inv = 1.0 / b
        c = pltpu.roll(a, n - s, 1)
        ka = -a * pltpu.roll(inv, s, 1)
        kc = -c * pltpu.roll(inv, n - s, 1)
        r = r + ka * pltpu.roll(r, s, 1) + kc * pltpu.roll(r, n - s, 1)
        b = b + ka * a + kc * c
        a = ka * pltpu.roll(a, s, 1)
    return r / b


def factor_kernel(nxd, si, zk, zib, ex, phx, psx, cx):
    kx = lax.axis_index("gx")
    nx, ny, nz = si.shape
    lane = iota(1, (ny, nz))
    for x in range(nx):
        a = jnp.where(lane == 0, 0.0, jnp.full((ny, nz), -1.0, F32))
        b = si[x] + jnp.where(lane == 0, 1.0, jnp.full((ny, nz), 2.0, F32))

        def store(level, ka, kc):
            zk[2 * level, x] = ka
            zk[2 * level + 1, x] = kc

        zib[x] = reduce_factors(a, b, 1, store)
    d = si[0] + jnp.where(kx == 0, 1.0, 2.0)
    r = jnp.full((ny, nz), jnp.where(kx == 0, 0.0, 1.0), F32)
    phx[0] = r
    for x in range(nx):
        e = 1.0 / d
        ex[x] = e
        if x < nx - 1:
            d = si[x + 1] + (2.0 - e)
            r = e * r
            phx[x + 1] = r
    u = ex[nx - 1] * r
    w = ex[nx - 1] * jnp.where(kx == nxd - 1, 0.0, 1.0)
    phx[nx - 1] = u
    psx[nx - 1] = w
    cx[2] = w
    for x in range(nx - 2, -1, -1):
        u = ex[x] * (phx[x] + u)
        w = ex[x] * w
        phx[x] = u
        psx[x] = w
    cx[0] = u
    cx[1] = w


def z_load(zk, x):
    return lambda level: (zk[2 * level, x], zk[2 * level + 1, x])


def chain_x_kernel(el, mg, ds, yk, yib, e1_up, iz_out, up_out, pair):
    nx, ny, nz = ds.shape
    for x in range(nx):
        above = el[1, x + 1] if x < nx - 1 else e1_up[0]
        iz = mg[2, x] - H * (above - el[1, x])
        iz_out[x] = iz
        h1 = mg[1, x]
        rhs = ds[x] * el[0, x] + ((iz - prev_y(iz, 0.0)) - (h1 - prev_z(h1))) * (1.0 / H)
        u = reduce_apply(rhs, 0, z_load(yk, x), yib[x])
        up_out[x] = u
        pair[0, x:x + 1] = u[0:1]
        pair[1, x:x + 1] = u[ny - 1:ny] - iz[ny - 1:ny] * (1.0 / H)


def chain_z_kernel(el, mg, ds, ex, halo_y, iy_out, up_out, pair):
    nx, ny, nz = ds.shape
    rhs = []
    below = jnp.zeros((ny, nz), F32)
    for x in range(nx):
        e0 = el[0, x]
        iy = mg[1, x] - H * (next_z(e0) - e0)
        iy_out[x] = iy
        h0 = mg[0, x]
        rhs.append(ds[x] * el[2, x] + ((iy - below) - (h0 - prev_y(h0, halo_y[0, x:x + 1]))) * (1.0 / H))
        below = iy
    sweep_x(rhs, ex, up_out)
    pair[0] = up_out[0]
    pair[1] = up_out[nx - 1] - below * (1.0 / H)


def center_y_kernel(el, mg, ds, zk, zib, halo_y, h2_low, sx_out, t1_out):
    nx, ny, nz = ds.shape
    for x in range(nx):
        e2 = el[2, x]
        ix = mg[0, x] - H * (next_y(e2, halo_y[1, x:x + 1]) - e2)
        below = mg[2, x - 1] if x > 0 else h2_low[0]
        rhs = ds[x] * el[1, x] + ((ix - prev_z(ix)) - (mg[2, x] - below)) * (1.0 / H)
        cy = reduce_apply(rhs, 1, z_load(zk, x), zib[x])
        curl = H * (next_z(cy) - cy)
        mx = ix + curl
        sx_out[x] = mx + curl
        t1_out[x] = ds[x] * cy + (mx - prev_z(mx)) * (1.0 / H)


def scan_y_kernel(ready, recv, own, pair, weights, consts, send, halo, mixed):
    ky = lax.axis_index("gy")
    n = recv.shape[0]
    halo[0] = jnp.where(ky == 0, 0.0, recv[jnp.maximum(ky - 1, 0), 3])
    halo[1] = jnp.where(ky == n - 1, 0.0, recv[jnp.minimum(ky + 1, n - 1), 3])
    interface_factors(lambda j: (recv[j, 0], recv[j, 1], recv[j, 2]), (own[0], own[1], own[2]),
                      n, ky, weights, mixed, consts)
    ready()
    fill_send(send, pair[0], pair[1], consts, n, ky)


def half_x_kernel(nxd, ready, recv, weights, consts, up, iz, t1, ds, phy, psy, ex, coef_x, pair_z, sz_out, t4_out, ufy_out, send, edge):
    ky = lax.axis_index("gy")
    nx, ny, nz = ds.shape
    A, C = gather_sums(recv, weights, recv.shape[0], ky)
    for x in range(nx):
        edge[0, x:x + 1] = up[x][0:1]
        edge[1, x:x + 1] = up[x][ny - 1:ny] - iz[x][ny - 1:ny] * (1.0 / H)
    lower, upper = boundary(A, C, edge[0], edge[1], consts)
    edge[0] = lower
    edge[1] = upper
    ready()
    rhs = []
    below = jnp.zeros((ny, nz), F32)
    for x in range(nx):
        lo = edge[0, x:x + 1]
        hi = edge[1, x:x + 1]
        cx = up[x] + phy[x] * lo + psy[x] * hi
        curl = H * (next_y(cx, hi) - cx)
        mz = iz[x] + curl
        sz = mz + curl
        sz_out[x] = sz
        mlow = jnp.where(ky == 0, 0.0, H * (cx[0:1] - lo))
        t4_out[x] = ds[x] * cx + (mz - prev_y(mz, mlow)) * (1.0 / H)
        rhs.append(t1[x] - (sz - below) * (1.0 / H))
        below = sz
    sweep_x(rhs, ex, ufy_out)
    f = ufy_out[0]
    l = ufy_out[nx - 1] + below * (1.0 / H)
    for j in range(nxd):
        for i in range(3):
            send[j, i] = coef_x[i]
        send[j, 3] = pair_z[0]
        send[j, 4] = pair_z[1]
        send[j, 5] = f
        send[j, 6] = l


def half_z_kernel(ready, recv, cx, pair_z, up, iy, sx, ufy, sz, ds, phx, psx, yk, yib, consts_y, sy_out, ufz_out, pair_out, edge_y_out, send, weights, mixed, consts):
    kx = lax.axis_index("gx")
    ky = lax.axis_index("gy")
    nx, ny, nz = ds.shape
    n = recv.shape[0]
    interface_factors(lambda j: (recv[j, 0], recv[j, 1], recv[j, 2]), (cx[0], cx[1], cx[2]), n, kx, weights, mixed, consts)
    A, C = gather_sums_pair(lambda j: (recv[j, 5], recv[j, 6]), weights, mixed, n, kx)
    ready()
    lower, upper = boundary(A, C, ufy[0], ufy[nx - 1] + sz[nx - 1] * (1.0 / H), consts)
    edge_y_out[0] = lower
    edge_y_out[1] = upper
    A, C = gather_sums_pair(lambda j: (recv[j, 3], recv[j, 4]), weights, mixed, n, kx)
    lower, upper = boundary(A, C, pair_z[0], pair_z[1], consts)
    cz = up[0] + phx[0] * lower + psx[0] * upper
    below = jnp.where(kx == 0, 0.0, H * (cz - lower))
    for x in range(nx):
        cn = up[x + 1] + phx[x + 1] * lower + psx[x + 1] * upper if x < nx - 1 else upper
        curl = H * (cn - cz)
        my = iy[x] + curl
        sy_out[x] = my + curl
        s = sx[x]
        rhs = ds[x] * cz + ((my - below) - (s - prev_y(s, 0.0))) * (1.0 / H)
        u = reduce_apply(rhs, 0, z_load(yk, x), yib[x])
        ufz_out[x] = u
        pair_out[0, x:x + 1] = u[0:1]
        pair_out[1, x:x + 1] = u[ny - 1:ny] + s[ny - 1:ny] * (1.0 / H)
        cz = cn
        below = my
    fill_send(send, pair_out[0], pair_out[1], consts_y, send.shape[0], ky)


def final_x_kernel(t4, sy, si, fx_out, my_out):
    nx = t4.shape[0]
    for x in range(nx):
        s = sy[x]
        fx = z_solve(si[x], t4[x] - (s - prev_z(s)) * (1.0 / H))
        fx_out[x] = fx
        my_out[x] = s - H * (next_z(fx) - fx)


def final_y_kernel(edge, up, sz, phx, psx, fy_out, mz_out):
    nx = up.shape[0]
    lower = edge[0]
    upper = edge[1]
    fy = up[0] + phx[0] * lower + psx[0] * upper
    for x in range(nx):
        fn = up[x + 1] + phx[x + 1] * lower + psx[x + 1] * upper if x < nx - 1 else upper
        fy_out[x] = fy
        mz_out[x] = sz[x] - H * (fn - fy)
        fy = fn


def final_z_kernel(ready, recv, weights, consts, pair, up, sx, phy, psy, fx, fy, my, mz, e_out, h_out, edge):
    ky = lax.axis_index("gy")
    nx = up.shape[0]
    A, C = gather_sums(recv, weights, recv.shape[0], ky)
    lower, upper = boundary(A, C, pair[0], pair[1], consts)
    ready()
    edge[0] = lower
    edge[1] = upper
    for x in range(nx):
        lo = edge[0, x:x + 1]
        hi = edge[1, x:x + 1]
        fz = up[x] + phy[x] * lo + psy[x] * hi
        e_out[0, x] = fx[x]
        e_out[1, x] = fy[x]
        e_out[2, x] = fz
        h_out[0, x] = sx[x] - H * (next_y(fz, hi) - fz)
        h_out[1, x] = my[x]
        h_out[2, x] = mz[x]


def staged(kernel, kinds_in, kinds_out, first):
    def body(*refs):
        ni = len(kinds_in)
        no = len(kinds_out)
        ins = refs[:ni]
        outs = refs[ni:ni + no]
        rest = list(refs[ni + no:])
        sems = rest.pop()
        work = []
        copies = []
        for ref, kind in zip(ins, kinds_in):
            if kind == "v":
                work.append(ref)
                continue
            held = rest.pop(0)
            copy = pltpu.make_async_copy(ref, held, sems.at[len(copies)])
            copy.start()
            copies.append(copy)
            work.append(held)
        back = []
        for ref, kind in zip(outs, kinds_out):
            if kind == "v":
                work.append(ref)
                continue
            held = rest.pop(0)
            back.append((held, ref))
            work.append(held)
        head = len(copies) if first is None else first
        for copy in copies[:head]:
            copy.wait()

        def ready():
            for copy in copies[head:]:
                copy.wait()

        if first is None:
            kernel(*work, *rest)
        else:
            kernel(ready, *work, *rest)
        copies = [pltpu.make_async_copy(held, ref, sems.at[i]) for i, (held, ref) in enumerate(back)]
        for copy in copies:
            copy.start()
        for copy in copies:
            copy.wait()

    return body


def call(kernel, outs, *args, smem=(), near=(), near_out=(), scratch=(), first=None, room=ROOM, hot=False, far=(), name=None):
    kinds_in = ["s" if i in smem else "v" if i in near or (hot and i not in far) else "h" for i in range(len(args))]
    kinds_out = ["v" if i in near_out or (hot and name.startswith(("final_x", "final_y"))) else "h" for i in range(len(outs))]
    held = []
    for a, kind in zip(args, kinds_in):
        if kind != "v":
            held.append((pltpu.SMEM if kind == "s" else pltpu.VMEM)(a.shape, a.dtype))
    for o, kind in zip(outs, kinds_out):
        if kind != "v":
            held.append(pltpu.VMEM(o, F32))
    spec = {"v": pltpu.VMEM, "h": HBM, "s": HBM}
    nbytes = sum(4 * _size(a.shape) for a in args) + sum(4 * _size(o) for o in outs)
    return pl.pallas_call(
        staged(kernel, kinds_in, kinds_out, 0 if hot and first is not None else first),
        out_shape=[jax.ShapeDtypeStruct(o, F32) for o in outs],
        in_specs=[pl.BlockSpec(memory_space=spec[k]) for k in kinds_in],
        out_specs=[pl.BlockSpec(memory_space=spec[k]) for k in kinds_out],
        scratch_shapes=held + list(scratch) + [pltpu.SemaphoreType.DMA((max(len(held), 1),))],
        cost_estimate=pl.CostEstimate(flops=4 * nbytes, bytes_accessed=nbytes, transcendentals=0),
        compiler_params=pltpu.CompilerParams(vmem_limit_bytes=room << 20),
        name=name,
    )(*args)


def _size(shape):
    n = 1
    for d in shape:
        n *= d
    return n


def shifted(array, axis, by):
    count = lax.axis_size(axis)
    return lax.ppermute(array, axis, [(i, i + by) for i in range(count) if 0 <= i + by < count])


def exchange(array, axis):
    return lax.all_to_all(array, axis, 0, 0)


def per_device(electric, magnetic, material, permittivity, conductivity):
    nxd = lax.axis_size("gx")
    nyd = lax.axis_size("gy")
    cell = material.shape
    nx, ny, nz = cell
    py = (nx, nz)
    px = (ny, nz)

    def bind(kernel, *lead):
        def body(*refs):
            kernel(*lead, *refs)
        return body


    ds, si, yk, yib, phy, psy, cy, send_c, pe1, ph2 = call(
        bind(coef_kernel, nyd),
        [cell, cell, (2 * len(strides(ny)),) + cell, cell, cell, cell, (3,) + py, (nyd, 4) + py,
         (1,) + px, (1,) + px],
        material, permittivity, conductivity, electric, magnetic, smem=(1, 2), first=3, room=60,
        scratch=[pltpu.VMEM(py, F32), pltpu.VMEM(py, F32)], name="coef")
    recv_c = exchange(send_c, "gy")
    e1_up = shifted(pe1, "gx", -1)
    h2_low = shifted(ph2, "gx", 1)
    zk, zib, ex, phx, psx, cx = call(
        bind(factor_kernel, nxd), [(2 * len(strides(nz)),) + cell, cell, cell, cell, cell, (3,) + px], si, name="factor")
    e1_up, h2_low, cx = lax.optimization_barrier((e1_up, h2_low, cx))
    iz, ux, pair_x = call(chain_x_kernel, [cell, cell, (2,) + py],
                          electric, magnetic, ds, yk, yib, e1_up, hot=True, far=(0, 1), room=40, name="chain_x")
    wy, ky, send1, halo_y = call(scan_y_kernel, [(nyd,) + py, (9,) + py, (nyd,) + py, (2,) + py], recv_c, cy, pair_x,
                         first=2, scratch=[pltpu.VMEM((nyd,) + py, F32)], hot=True, room=40, name="scan_y")
    recv1 = exchange(send1, "gy")

    iy, uz, pair_z = call(chain_z_kernel, [cell, cell, (2,) + px], electric, magnetic, ds, ex, halo_y, name="chain_z")
    sx, t1 = call(center_y_kernel, [cell, cell], electric, magnetic, ds, zk, zib, halo_y, h2_low, name="center_y")

    sz, t4, ufy, send2 = call(
        bind(half_x_kernel, nxd), [cell, cell, cell, (nxd, 7) + px],
        recv1, wy, ky, ux, iz, t1, ds, phy, psy, ex, cx, pair_z,
        first=4, scratch=[pltpu.VMEM((2,) + py, F32)], hot=True, room=40, name="half_x")
    recv2 = exchange(send2, "gx")
    sy, ufz, pair4, edge_y, send3 = call(
        half_z_kernel, [cell, cell, (2,) + py, (2,) + px, (nyd,) + py],
        recv2, cx, pair_z, uz, iy, sx, ufy, sz, ds, phx, psx, yk, yib, ky,
        first=2, scratch=[pltpu.VMEM((nxd,) + px, F32), pltpu.VMEM((nxd,) + px, F32), pltpu.VMEM((9,) + px, F32)],
        hot=True, room=40, name="half_z")
    recv3 = exchange(send3, "gy")
    fx, my = call(final_x_kernel, [cell, cell], t4, sy, si, hot=True, room=40, name="final_x")
    fy, mz = call(final_y_kernel, [cell, cell], edge_y, ufy, sz, phx, psx, hot=True, room=40, name="final_y")
    e, h = call(final_z_kernel, [(3,) + cell, (3,) + cell],
                recv3, wy, ky, pair4, ufz, sx, phy, psy, fx, fy, my, mz,
                first=4, scratch=[pltpu.VMEM((2,) + py, F32)], hot=True, room=40, name="final_z")
    return e, h


def solution(mesh):
    return jax.shard_map(
        per_device,
        mesh=mesh,
        in_specs=(
            P(None, "gx", "gy", None),
            P(None, "gx", "gy", None),
            P("gx", "gy", None),
            P(),
            P(),
        ),
        out_specs=(P(None, "gx", "gy", None), P(None, "gx", "gy", None)),
        check_vma=False,
    )
```

```python
import jax
import jax.numpy as jnp
from jax import lax
from jax.experimental import pallas as pl
from jax.experimental.pallas import tpu as pltpu
from jax.sharding import PartitionSpec as P

H = 12.0
F32 = jnp.float32
HBM = pltpu.HBM
ROOM = 60


def iota(axis, shape):
    return lax.broadcasted_iota(jnp.int32, shape, axis)


def next_z(v):
    n = v.shape[1]
    return jnp.where(iota(1, v.shape) == n - 1, 0.0, pltpu.roll(v, n - 1, 1))


def prev_z(v):
    return jnp.where(iota(1, v.shape) == 0, 0.0, pltpu.roll(v, 1, 1))


def next_y(v, row):
    n = v.shape[0]
    return jnp.where(iota(0, v.shape) == n - 1, row, pltpu.roll(v, n - 1, 0))


def prev_y(v, row):
    return jnp.where(iota(0, v.shape) == 0, row, pltpu.roll(v, 1, 0))


def strides(n):
    out = []
    s = 1
    while s < n:
        out.append(s)
        s *= 2
    return out


def reduce_factors(a, b, axis, store):
    n = a.shape[axis]
    for level, s in enumerate(strides(n)):
        inv = 1.0 / b
        c = pltpu.roll(a, n - s, axis)
        ka = -a * pltpu.roll(inv, s, axis)
        kc = -c * pltpu.roll(inv, n - s, axis)
        store(level, ka, kc)
        b = b + ka * a + kc * c
        a = ka * pltpu.roll(a, s, axis)
    return 1.0 / b


def reduce_apply(r, axis, load, inv):
    n = r.shape[axis]
    for level, s in enumerate(strides(n)):
        ka, kc = load(level)
        r = r + ka * pltpu.roll(r, s, axis) + kc * pltpu.roll(r, n - s, axis)
    return r * inv


def sweep_x(rhs, ex, out):
    nx = len(rhs)
    fwd = [rhs[0]]
    for i in range(1, nx):
        fwd.append(rhs[i] + ex[i - 1] * fwd[i - 1])
    u = ex[nx - 1] * fwd[nx - 1]
    out[nx - 1] = u
    for i in range(nx - 2, -1, -1):
        u = ex[i] * (fwd[i] + u)
        out[i] = u


def interface_factors(coef, own, n, k, weights, mixed, consts):
    zero = jnp.zeros_like(own[0])
    B = zero
    for j in range(n - 1):
        al, be, de = coef(j)
        g = be / (1.0 - al * B)
        h = g * B
        weights[j] = g
        mixed[j] = h
        B = jnp.where(j < k, de + h * be, B)
    D = zero
    for j in range(n - 1, 0, -1):
        al, be, de = coef(j)
        g = be / (1.0 - de * D)
        h = g * D
        weights[j] = jnp.where(j > k, g, weights[j]) if j < n - 1 else g
        mixed[j] = jnp.where(j > k, h, mixed[j]) if j < n - 1 else h
        D = jnp.where(j > k, al + h * be, D)
    al, be, de = own
    den = 1.0 / (1.0 - al * B)
    gl = be * den
    bp = de + gl * be * B
    consts[0] = gl * B
    consts[1] = be * D / (1.0 - de * D)
    consts[2] = gl
    consts[3] = bp
    consts[4] = 1.0 / (1.0 - bp * D)
    consts[5] = D
    consts[6] = den
    consts[7] = den * al
    consts[8] = B


def to_right(f, l, consts):
    return l + consts[0] * f


def to_left(f, l, consts):
    return f + consts[1] * l


def boundary(A, C, f, l, consts):
    v = (to_right(f, l, consts) + consts[2] * A + consts[3] * C) * consts[4]
    upper = C + consts[5] * v
    first = consts[6] * f + consts[7] * A + consts[2] * upper
    lower = A + consts[8] * first
    return lower, upper


def gather_sums(recv, weights, n, k):
    A = jnp.zeros_like(recv[0])
    for j in range(n - 1):
        A = jnp.where(j < k, recv[j] + weights[j] * A, A)
    C = jnp.zeros_like(A)
    for j in range(n - 1, 0, -1):
        C = jnp.where(j > k, recv[j] + weights[j] * C, C)
    return A, C


def gather_sums_pair(pair, weights, mixed, n, k):
    A = jnp.zeros_like(weights[0])
    for j in range(n - 1):
        f, l = pair(j)
        A = jnp.where(j < k, l + mixed[j] * f + weights[j] * A, A)
    C = jnp.zeros_like(A)
    for j in range(n - 1, 0, -1):
        f, l = pair(j)
        C = jnp.where(j > k, f + mixed[j] * l + weights[j] * C, C)
    return A, C


def fill_send(send, f, l, consts, n, k):
    right = to_right(f, l, consts)
    left = to_left(f, l, consts)
    for j in range(n):
        send[j] = jnp.where(j > k, right, left)


def y_factors(si, ky):
    row = iota(0, si.shape)
    zero = jnp.zeros(si.shape, F32)
    a = jnp.where(row == 0, 0.0, zero - 1.0)
    b = si + jnp.where(row == 0, jnp.where(ky == 0, 1.0, 2.0), 2.0)
    kept = []
    inv = reduce_factors(a, b, 0, lambda level, ka, kc: kept.append((ka, kc)))
    return kept, inv


def coef_kernel(nyd, ready, mat, perm, cond, el, mg, ds, si, phy, psy, cy, send, pe1, ph2, pe2, ph0):
    ky = lax.axis_index("gy")
    nx, ny, nz = mat.shape
    row = iota(0, (ny, nz))
    for x in range(nx):
        m = mat[x]
        eps = jnp.full(m.shape, perm[0], F32)
        sig = jnp.full(m.shape, cond[0], F32)
        for t in range(1, perm.shape[0]):
            eps = jnp.where(m == t, perm[t], eps)
            sig = jnp.where(m == t, cond[t], sig)
        ea = eps * (1.0 / (H * H))
        sh = sig * (0.5 / H)
        ds[x] = ea - sh
        inv_s = ea + sh
        si[x] = inv_s
        first = row == 0
        last = row == ny - 1
        a = jnp.where(first, 0.0, jnp.full(m.shape, -1.0, F32))
        b = inv_s + jnp.where(first, jnp.where(ky == 0, 1.0, 2.0), 2.0)

        kept = []
        ib = reduce_factors(a, b, 0, lambda level, ka, kc: kept.append((ka, kc)))
        load = kept.__getitem__
        lo = reduce_apply(jnp.where(first, jnp.where(ky == 0, 0.0, 1.0), jnp.zeros(m.shape, F32)), 0, load, ib)
        up = reduce_apply(jnp.where(last, jnp.where(ky == nyd - 1, 0.0, 1.0), jnp.zeros(m.shape, F32)), 0, load, ib)
        phy[x] = lo
        psy[x] = up
        cy[0, x:x + 1] = lo[0:1]
        cy[1, x:x + 1] = up[0:1]
        cy[2, x:x + 1] = up[ny - 1:ny]
    for j in range(nyd):
        send[j, 0:3] = cy[...]
    ready()
    pe1[0] = el[1, 0]
    ph2[0] = mg[2, nx - 1]
    for x in range(nx):
        pe2[x:x + 1] = el[2, x][0:1]
        ph0[x:x + 1] = mg[0, x][ny - 1:ny]
    for j in range(nyd):
        send[j, 3] = jnp.where(j > ky, ph0[...], pe2[...])


def z_solve(si, rhs):
    n = rhs.shape[1]
    lane = iota(1, rhs.shape)
    a = jnp.where(lane == 0, 0.0, jnp.full(rhs.shape, -1.0, F32))
    b = si + jnp.where(lane == 0, 1.0, jnp.full(rhs.shape, 2.0, F32))
    r = rhs
    for s in strides(n):
        inv = 1.0 / b
        c = pltpu.roll(a, n - s, 1)
        ka = -a * pltpu.roll(inv, s, 1)
        kc = -c * pltpu.roll(inv, n - s, 1)
        r = r + ka * pltpu.roll(r, s, 1) + kc * pltpu.roll(r, n - s, 1)
        b = b + ka * a + kc * c
        a = ka * pltpu.roll(a, s, 1)
    return r / b


def factor_kernel(nxd, si, zk, zib, ex, phx, psx, cx):
    kx = lax.axis_index("gx")
    nx, ny, nz = si.shape
    lane = iota(1, (ny, nz))
    for x in range(nx):
        a = jnp.where(lane == 0, 0.0, jnp.full((ny, nz), -1.0, F32))
        b = si[x] + jnp.where(lane == 0, 1.0, jnp.full((ny, nz), 2.0, F32))

        def store(level, ka, kc):
            zk[2 * level, x] = ka
            zk[2 * level + 1, x] = kc

        zib[x] = reduce_factors(a, b, 1, store)
    d = si[0] + jnp.where(kx == 0, 1.0, 2.0)
    r = jnp.full((ny, nz), jnp.where(kx == 0, 0.0, 1.0), F32)
    phx[0] = r
    for x in range(nx):
        e = 1.0 / d
        ex[x] = e
        if x < nx - 1:
            d = si[x + 1] + (2.0 - e)
            r = e * r
            phx[x + 1] = r
    u = ex[nx - 1] * r
    w = ex[nx - 1] * jnp.where(kx == nxd - 1, 0.0, 1.0)
    phx[nx - 1] = u
    psx[nx - 1] = w
    cx[2] = w
    for x in range(nx - 2, -1, -1):
        u = ex[x] * (phx[x] + u)
        w = ex[x] * w
        phx[x] = u
        psx[x] = w
    cx[0] = u
    cx[1] = w


def z_load(zk, x):
    return lambda level: (zk[2 * level, x], zk[2 * level + 1, x])


def chain_x_kernel(el, mg, ds, si, e1_up, iz_out, up_out, pair):
    ky = lax.axis_index("gy")
    nx, ny, nz = ds.shape
    for x in range(nx):
        above = el[1, x + 1] if x < nx - 1 else e1_up[0]
        iz = mg[2, x] - H * (above - el[1, x])
        iz_out[x] = iz
        h1 = mg[1, x]
        rhs = ds[x] * el[0, x] + ((iz - prev_y(iz, 0.0)) - (h1 - prev_z(h1))) * (1.0 / H)
        kept, inv = y_factors(si[x], ky)
        u = reduce_apply(rhs, 0, kept.__getitem__, inv)
        up_out[x] = u
        pair[0, x:x + 1] = u[0:1]
        pair[1, x:x + 1] = u[ny - 1:ny] - iz[ny - 1:ny] * (1.0 / H)


def chain_z_kernel(el, mg, ds, ex, halo_y, iy_out, up_out, pair):
    nx, ny, nz = ds.shape
    rhs = []
    below = jnp.zeros((ny, nz), F32)
    for x in range(nx):
        e0 = el[0, x]
        iy = mg[1, x] - H * (next_z(e0) - e0)
        iy_out[x] = iy
        h0 = mg[0, x]
        rhs.append(ds[x] * el[2, x] + ((iy - below) - (h0 - prev_y(h0, halo_y[0, x:x + 1]))) * (1.0 / H))
        below = iy
    sweep_x(rhs, ex, up_out)
    pair[0] = up_out[0]
    pair[1] = up_out[nx - 1] - below * (1.0 / H)


def center_y_kernel(el, mg, ds, zk, zib, halo_y, h2_low, sx_out, t1_out):
    nx, ny, nz = ds.shape
    for x in range(nx):
        e2 = el[2, x]
        ix = mg[0, x] - H * (next_y(e2, halo_y[1, x:x + 1]) - e2)
        below = mg[2, x - 1] if x > 0 else h2_low[0]
        rhs = ds[x] * el[1, x] + ((ix - prev_z(ix)) - (mg[2, x] - below)) * (1.0 / H)
        cy = reduce_apply(rhs, 1, z_load(zk, x), zib[x])
        curl = H * (next_z(cy) - cy)
        mx = ix + curl
        sx_out[x] = mx + curl
        t1_out[x] = ds[x] * cy + (mx - prev_z(mx)) * (1.0 / H)


def scan_y_kernel(ready, recv, own, pair, weights, consts, send, halo, mixed):
    ky = lax.axis_index("gy")
    n = recv.shape[0]
    halo[0] = jnp.where(ky == 0, 0.0, recv[jnp.maximum(ky - 1, 0), 3])
    halo[1] = jnp.where(ky == n - 1, 0.0, recv[jnp.minimum(ky + 1, n - 1), 3])
    interface_factors(lambda j: (recv[j, 0], recv[j, 1], recv[j, 2]), (own[0], own[1], own[2]),
                      n, ky, weights, mixed, consts)
    ready()
    fill_send(send, pair[0], pair[1], consts, n, ky)


def half_x_kernel(nxd, ready, recv, weights, consts, up, iz, t1, ds, phy, psy, ex, coef_x, pair_z, sz_out, t4_out, ufy_out, send, edge):
    ky = lax.axis_index("gy")
    nx, ny, nz = ds.shape
    A, C = gather_sums(recv, weights, recv.shape[0], ky)
    for x in range(nx):
        edge[0, x:x + 1] = up[x][0:1]
        edge[1, x:x + 1] = up[x][ny - 1:ny] - iz[x][ny - 1:ny] * (1.0 / H)
    lower, upper = boundary(A, C, edge[0], edge[1], consts)
    edge[0] = lower
    edge[1] = upper
    ready()
    rhs = []
    below = jnp.zeros((ny, nz), F32)
    for x in range(nx):
        lo = edge[0, x:x + 1]
        hi = edge[1, x:x + 1]
        cx = up[x] + phy[x] * lo + psy[x] * hi
        curl = H * (next_y(cx, hi) - cx)
        mz = iz[x] + curl
        sz = mz + curl
        sz_out[x] = sz
        mlow = jnp.where(ky == 0, 0.0, H * (cx[0:1] - lo))
        t4_out[x] = ds[x] * cx + (mz - prev_y(mz, mlow)) * (1.0 / H)
        rhs.append(t1[x] - (sz - below) * (1.0 / H))
        below = sz
    sweep_x(rhs, ex, ufy_out)
    f = ufy_out[0]
    l = ufy_out[nx - 1] + below * (1.0 / H)
    for j in range(nxd):
        for i in range(3):
            send[j, i] = coef_x[i]
        send[j, 3] = pair_z[0]
        send[j, 4] = pair_z[1]
        send[j, 5] = f
        send[j, 6] = l


def half_z_kernel(ready, recv, cx, pair_z, up, iy, sx, ufy, sz, ds, phx, psx, si, consts_y, sy_out, ufz_out, pair_out, edge_y_out, send, weights, mixed, consts):
    kx = lax.axis_index("gx")
    ky = lax.axis_index("gy")
    nx, ny, nz = ds.shape
    n = recv.shape[0]
    interface_factors(lambda j: (recv[j, 0], recv[j, 1], recv[j, 2]), (cx[0], cx[1], cx[2]), n, kx, weights, mixed, consts)
    A, C = gather_sums_pair(lambda j: (recv[j, 5], recv[j, 6]), weights, mixed, n, kx)
    ready()
    lower, upper = boundary(A, C, ufy[0], ufy[nx - 1] + sz[nx - 1] * (1.0 / H), consts)
    edge_y_out[0] = lower
    edge_y_out[1] = upper
    A, C = gather_sums_pair(lambda j: (recv[j, 3], recv[j, 4]), weights, mixed, n, kx)
    lower, upper = boundary(A, C, pair_z[0], pair_z[1], consts)
    cz = up[0] + phx[0] * lower + psx[0] * upper
    below = jnp.where(kx == 0, 0.0, H * (cz - lower))
    for x in range(nx):
        cn = up[x + 1] + phx[x + 1] * lower + psx[x + 1] * upper if x < nx - 1 else upper
        curl = H * (cn - cz)
        my = iy[x] + curl
        sy_out[x] = my + curl
        s = sx[x]
        rhs = ds[x] * cz + ((my - below) - (s - prev_y(s, 0.0))) * (1.0 / H)
        kept, inv = y_factors(si[x], ky)
        u = reduce_apply(rhs, 0, kept.__getitem__, inv)
        ufz_out[x] = u
        pair_out[0, x:x + 1] = u[0:1]
        pair_out[1, x:x + 1] = u[ny - 1:ny] + s[ny - 1:ny] * (1.0 / H)
        cz = cn
        below = my
    fill_send(send, pair_out[0], pair_out[1], consts_y, send.shape[0], ky)


def final_x_kernel(t4, sy, si, fx_out, my_out):
    nx = t4.shape[0]
    for x in range(nx):
        s = sy[x]
        fx = z_solve(si[x], t4[x] - (s - prev_z(s)) * (1.0 / H))
        fx_out[x] = fx
        my_out[x] = s - H * (next_z(fx) - fx)


def final_y_kernel(edge, up, sz, phx, psx, fy_out, mz_out):
    nx = up.shape[0]
    lower = edge[0]
    upper = edge[1]
    fy = up[0] + phx[0] * lower + psx[0] * upper
    for x in range(nx):
        fn = up[x + 1] + phx[x + 1] * lower + psx[x + 1] * upper if x < nx - 1 else upper
        fy_out[x] = fy
        mz_out[x] = sz[x] - H * (fn - fy)
        fy = fn


def final_z_kernel(ready, recv, weights, consts, pair, up, sx, phy, psy, fx, fy, my, mz, e_out, h_out, edge):
    ky = lax.axis_index("gy")
    nx = up.shape[0]
    A, C = gather_sums(recv, weights, recv.shape[0], ky)
    lower, upper = boundary(A, C, pair[0], pair[1], consts)
    ready()
    edge[0] = lower
    edge[1] = upper
    for x in range(nx):
        lo = edge[0, x:x + 1]
        hi = edge[1, x:x + 1]
        fz = up[x] + phy[x] * lo + psy[x] * hi
        e_out[0, x] = fx[x]
        e_out[1, x] = fy[x]
        e_out[2, x] = fz
        h_out[0, x] = sx[x] - H * (next_y(fz, hi) - fz)
        h_out[1, x] = my[x]
        h_out[2, x] = mz[x]


def staged(kernel, kinds_in, kinds_out, first):
    def body(*refs):
        ni = len(kinds_in)
        no = len(kinds_out)
        ins = refs[:ni]
        outs = refs[ni:ni + no]
        rest = list(refs[ni + no:])
        sems = rest.pop()
        work = []
        copies = []
        for ref, kind in zip(ins, kinds_in):
            if kind == "v":
                work.append(ref)
                continue
            held = rest.pop(0)
            copy = pltpu.make_async_copy(ref, held, sems.at[len(copies)])
            copy.start()
            copies.append(copy)
            work.append(held)
        back = []
        for ref, kind in zip(outs, kinds_out):
            if kind == "v":
                work.append(ref)
                continue
            held = rest.pop(0)
            back.append((held, ref))
            work.append(held)
        head = len(copies) if first is None else first
        for copy in copies[:head]:
            copy.wait()

        def ready():
            for copy in copies[head:]:
                copy.wait()

        if first is None:
            kernel(*work, *rest)
        else:
            kernel(ready, *work, *rest)
        copies = [pltpu.make_async_copy(held, ref, sems.at[i]) for i, (held, ref) in enumerate(back)]
        for copy in copies:
            copy.start()
        for copy in copies:
            copy.wait()

    return body


def call(kernel, outs, *args, smem=(), near=(), near_out=(), scratch=(), first=None, room=ROOM, hot=False, far=(), name=None):
    kinds_in = ["s" if i in smem else "v" if i in near or (hot and i not in far) else "h" for i in range(len(args))]
    kinds_out = ["v" if i in near_out or (hot and name.startswith(("final_x", "final_y"))) else "h" for i in range(len(outs))]
    held = []
    for a, kind in zip(args, kinds_in):
        if kind != "v":
            held.append((pltpu.SMEM if kind == "s" else pltpu.VMEM)(a.shape, a.dtype))
    for o, kind in zip(outs, kinds_out):
        if kind != "v":
            held.append(pltpu.VMEM(o, F32))
    spec = {"v": pltpu.VMEM, "h": HBM, "s": HBM}
    nbytes = sum(4 * _size(a.shape) for a in args) + sum(4 * _size(o) for o in outs)
    return pl.pallas_call(
        staged(kernel, kinds_in, kinds_out, 0 if hot and first is not None else first),
        out_shape=[jax.ShapeDtypeStruct(o, F32) for o in outs],
        in_specs=[pl.BlockSpec(memory_space=spec[k]) for k in kinds_in],
        out_specs=[pl.BlockSpec(memory_space=spec[k]) for k in kinds_out],
        scratch_shapes=held + list(scratch) + [pltpu.SemaphoreType.DMA((max(len(held), 1),))],
        cost_estimate=pl.CostEstimate(flops=4 * nbytes, bytes_accessed=nbytes, transcendentals=0),
        compiler_params=pltpu.CompilerParams(vmem_limit_bytes=room << 20),
        name=name,
    )(*args)


def _size(shape):
    n = 1
    for d in shape:
        n *= d
    return n


def shifted(array, axis, by):
    count = lax.axis_size(axis)
    return lax.ppermute(array, axis, [(i, i + by) for i in range(count) if 0 <= i + by < count])


def exchange(array, axis):
    return lax.all_to_all(array, axis, 0, 0)


def per_device(electric, magnetic, material, permittivity, conductivity):
    nxd = lax.axis_size("gx")
    nyd = lax.axis_size("gy")
    cell = material.shape
    nx, ny, nz = cell
    py = (nx, nz)
    px = (ny, nz)

    def bind(kernel, *lead):
        def body(*refs):
            kernel(*lead, *refs)
        return body


    ds, si, phy, psy, cy, send_c, pe1, ph2 = call(
        bind(coef_kernel, nyd),
        [cell, cell, cell, cell, (3,) + py, (nyd, 4) + py,
         (1,) + px, (1,) + px],
        material, permittivity, conductivity, electric, magnetic, smem=(1, 2), first=3, room=60,
        scratch=[pltpu.VMEM(py, F32), pltpu.VMEM(py, F32)], name="coef")
    recv_c = exchange(send_c, "gy")
    e1_up = shifted(pe1, "gx", -1)
    h2_low = shifted(ph2, "gx", 1)
    zk, zib, ex, phx, psx, cx = call(
        bind(factor_kernel, nxd), [(2 * len(strides(nz)),) + cell, cell, cell, cell, cell, (3,) + px], si, name="factor")
    e1_up, h2_low, cx = lax.optimization_barrier((e1_up, h2_low, cx))
    iz, ux, pair_x = call(chain_x_kernel, [cell, cell, (2,) + py],
                          electric, magnetic, ds, si, e1_up, hot=True, far=(0, 1), room=40, name="chain_x")
    wy, ky, send1, halo_y = call(scan_y_kernel, [(nyd,) + py, (9,) + py, (nyd,) + py, (2,) + py], recv_c, cy, pair_x,
                         first=2, scratch=[pltpu.VMEM((nyd,) + py, F32)], hot=True, room=40, name="scan_y")
    recv1 = exchange(send1, "gy")

    iy, uz, pair_z = call(chain_z_kernel, [cell, cell, (2,) + px], electric, magnetic, ds, ex, halo_y, name="chain_z")
    sx, t1 = call(center_y_kernel, [cell, cell], electric, magnetic, ds, zk, zib, halo_y, h2_low, name="center_y")

    sz, t4, ufy, send2 = call(
        bind(half_x_kernel, nxd), [cell, cell, cell, (nxd, 7) + px],
        recv1, wy, ky, ux, iz, t1, ds, phy, psy, ex, cx, pair_z,
        first=4, scratch=[pltpu.VMEM((2,) + py, F32)], hot=True, room=40, name="half_x")
    recv2 = exchange(send2, "gx")
    sy, ufz, pair4, edge_y, send3 = call(
        half_z_kernel, [cell, cell, (2,) + py, (2,) + px, (nyd,) + py],
        recv2, cx, pair_z, uz, iy, sx, ufy, sz, ds, phx, psx, si, ky,
        first=2, scratch=[pltpu.VMEM((nxd,) + px, F32), pltpu.VMEM((nxd,) + px, F32), pltpu.VMEM((9,) + px, F32)],
        hot=True, room=40, name="half_z")
    recv3 = exchange(send3, "gy")
    fx, my = call(final_x_kernel, [cell, cell], t4, sy, si, hot=True, room=40, name="final_x")
    fy, mz = call(final_y_kernel, [cell, cell], edge_y, ufy, sz, phx, psx, hot=True, room=40, name="final_y")
    e, h = call(final_z_kernel, [(3,) + cell, (3,) + cell],
                recv3, wy, ky, pair4, ufz, sx, phy, psy, fx, fy, my, mz,
                first=4, scratch=[pltpu.VMEM((2,) + py, F32)], hot=True, room=40, name="final_z")
    return e, h


def solution(mesh):
    return jax.shard_map(
        per_device,
        mesh=mesh,
        in_specs=(
            P(None, "gx", "gy", None),
            P(None, "gx", "gy", None),
            P("gx", "gy", None),
            P(),
            P(),
        ),
        out_specs=(P(None, "gx", "gy", None), P(None, "gx", "gy", None)),
        check_vma=False,
    )
```

```python
import jax
import jax.numpy as jnp
from jax import lax
from jax.experimental import pallas as pl
from jax.experimental.pallas import tpu as pltpu
from jax.sharding import PartitionSpec as P

H = 12.0
F32 = jnp.float32
HBM = pltpu.HBM
ROOM = 60


def iota(axis, shape):
    return lax.broadcasted_iota(jnp.int32, shape, axis)


def next_z(v):
    n = v.shape[1]
    return jnp.where(iota(1, v.shape) == n - 1, 0.0, pltpu.roll(v, n - 1, 1))


def prev_z(v):
    return jnp.where(iota(1, v.shape) == 0, 0.0, pltpu.roll(v, 1, 1))


def next_y(v, row):
    n = v.shape[0]
    return jnp.where(iota(0, v.shape) == n - 1, row, pltpu.roll(v, n - 1, 0))


def prev_y(v, row):
    return jnp.where(iota(0, v.shape) == 0, row, pltpu.roll(v, 1, 0))


def strides(n):
    out = []
    s = 1
    while s < n:
        out.append(s)
        s *= 2
    return out


def reduce_factors(a, b, axis, store):
    n = a.shape[axis]
    for level, s in enumerate(strides(n)):
        inv = 1.0 / b
        c = pltpu.roll(a, n - s, axis)
        ka = -a * pltpu.roll(inv, s, axis)
        kc = -c * pltpu.roll(inv, n - s, axis)
        store(level, ka, kc)
        b = b + ka * a + kc * c
        a = ka * pltpu.roll(a, s, axis)
    return 1.0 / b


def reduce_apply(r, axis, load, inv):
    n = r.shape[axis]
    for level, s in enumerate(strides(n)):
        ka, kc = load(level)
        r = r + ka * pltpu.roll(r, s, axis) + kc * pltpu.roll(r, n - s, axis)
    return r * inv


def sweep_x(rhs, ex, out):
    nx = len(rhs)
    fwd = [rhs[0]]
    for i in range(1, nx):
        fwd.append(rhs[i] + ex[i - 1] * fwd[i - 1])
    u = ex[nx - 1] * fwd[nx - 1]
    out[nx - 1] = u
    for i in range(nx - 2, -1, -1):
        u = ex[i] * (fwd[i] + u)
        out[i] = u


def interface_factors(coef, own, n, k, weights, mixed, consts):
    zero = jnp.zeros_like(own[0])
    B = zero
    for j in range(n - 1):
        al, be, de = coef(j)
        g = be / (1.0 - al * B)
        h = g * B
        weights[j] = g
        mixed[j] = h
        B = jnp.where(j < k, de + h * be, B)
    D = zero
    for j in range(n - 1, 0, -1):
        al, be, de = coef(j)
        g = be / (1.0 - de * D)
        h = g * D
        weights[j] = jnp.where(j > k, g, weights[j]) if j < n - 1 else g
        mixed[j] = jnp.where(j > k, h, mixed[j]) if j < n - 1 else h
        D = jnp.where(j > k, al + h * be, D)
    al, be, de = own
    den = 1.0 / (1.0 - al * B)
    gl = be * den
    bp = de + gl * be * B
    consts[0] = gl * B
    consts[1] = be * D / (1.0 - de * D)
    consts[2] = gl
    consts[3] = bp
    consts[4] = 1.0 / (1.0 - bp * D)
    consts[5] = D
    consts[6] = den
    consts[7] = den * al
    consts[8] = B


def to_right(f, l, consts):
    return l + consts[0] * f


def to_left(f, l, consts):
    return f + consts[1] * l


def boundary(A, C, f, l, consts):
    v = (to_right(f, l, consts) + consts[2] * A + consts[3] * C) * consts[4]
    upper = C + consts[5] * v
    first = consts[6] * f + consts[7] * A + consts[2] * upper
    lower = A + consts[8] * first
    return lower, upper


def gather_sums(recv, weights, n, k):
    A = jnp.zeros_like(recv[0])
    for j in range(n - 1):
        A = jnp.where(j < k, recv[j] + weights[j] * A, A)
    C = jnp.zeros_like(A)
    for j in range(n - 1, 0, -1):
        C = jnp.where(j > k, recv[j] + weights[j] * C, C)
    return A, C


def gather_sums_pair(pair, weights, mixed, n, k):
    A = jnp.zeros_like(weights[0])
    for j in range(n - 1):
        f, l = pair(j)
        A = jnp.where(j < k, l + mixed[j] * f + weights[j] * A, A)
    C = jnp.zeros_like(A)
    for j in range(n - 1, 0, -1):
        f, l = pair(j)
        C = jnp.where(j > k, f + mixed[j] * l + weights[j] * C, C)
    return A, C


def fill_send(send, f, l, consts, n, k):
    right = to_right(f, l, consts)
    left = to_left(f, l, consts)
    for j in range(n):
        send[j] = jnp.where(j > k, right, left)


def y_factors(si, ky):
    row = iota(0, si.shape)
    zero = jnp.zeros(si.shape, F32)
    a = jnp.where(row == 0, 0.0, zero - 1.0)
    b = si + jnp.where(row == 0, jnp.where(ky == 0, 1.0, 2.0), 2.0)
    kept = []
    inv = reduce_factors(a, b, 0, lambda level, ka, kc: kept.append((ka, kc)))
    return kept, inv


def coef_kernel(nyd, ready, mat, perm, cond, el, mg, ds, si, phy, psy, cy, send, pe1, ph2, pe2, ph0):
    ky = lax.axis_index("gy")
    nx, ny, nz = mat.shape
    row = iota(0, (ny, nz))
    for x in range(nx):
        m = mat[x]
        eps = jnp.full(m.shape, perm[0], F32)
        sig = jnp.full(m.shape, cond[0], F32)
        for t in range(1, perm.shape[0]):
            eps = jnp.where(m == t, perm[t], eps)
            sig = jnp.where(m == t, cond[t], sig)
        ea = eps * (1.0 / (H * H))
        sh = sig * (0.5 / H)
        ds[x] = ea - sh
        inv_s = ea + sh
        si[x] = inv_s
        first = row == 0
        last = row == ny - 1
        a = jnp.where(first, 0.0, jnp.full(m.shape, -1.0, F32))
        b = inv_s + jnp.where(first, jnp.where(ky == 0, 1.0, 2.0), 2.0)

        kept = []
        ib = reduce_factors(a, b, 0, lambda level, ka, kc: kept.append((ka, kc)))
        load = kept.__getitem__
        lo = reduce_apply(jnp.where(first, jnp.where(ky == 0, 0.0, 1.0), jnp.zeros(m.shape, F32)), 0, load, ib)
        up = reduce_apply(jnp.where(last, jnp.where(ky == nyd - 1, 0.0, 1.0), jnp.zeros(m.shape, F32)), 0, load, ib)
        phy[x] = lo
        psy[x] = up
        cy[0, x:x + 1] = lo[0:1]
        cy[1, x:x + 1] = up[0:1]
        cy[2, x:x + 1] = up[ny - 1:ny]
    for j in range(nyd):
        send[j, 0:3] = cy[...]
    ready()
    pe1[0] = el[1, 0]
    ph2[0] = mg[2, nx - 1]
    for x in range(nx):
        pe2[x:x + 1] = el[2, x][0:1]
        ph0[x:x + 1] = mg[0, x][ny - 1:ny]
    for j in range(nyd):
        send[j, 3] = jnp.where(j > ky, ph0[...], pe2[...])


def z_solve(si, rhs):
    n = rhs.shape[1]
    lane = iota(1, rhs.shape)
    a = jnp.where(lane == 0, 0.0, jnp.full(rhs.shape, -1.0, F32))
    b = si + jnp.where(lane == 0, 1.0, jnp.full(rhs.shape, 2.0, F32))
    r = rhs
    for s in strides(n):
        inv = 1.0 / b
        c = pltpu.roll(a, n - s, 1)
        ka = -a * pltpu.roll(inv, s, 1)
        kc = -c * pltpu.roll(inv, n - s, 1)
        r = r + ka * pltpu.roll(r, s, 1) + kc * pltpu.roll(r, n - s, 1)
        b = b + ka * a + kc * c
        a = ka * pltpu.roll(a, s, 1)
    return r / b


def factor_kernel(nxd, si, zk, zib, ex, phx, psx, cx):
    kx = lax.axis_index("gx")
    nx, ny, nz = si.shape
    lane = iota(1, (ny, nz))
    for x in range(nx):
        a = jnp.where(lane == 0, 0.0, jnp.full((ny, nz), -1.0, F32))
        b = si[x] + jnp.where(lane == 0, 1.0, jnp.full((ny, nz), 2.0, F32))

        def store(level, ka, kc):
            zk[2 * level, x] = ka
            zk[2 * level + 1, x] = kc

        zib[x] = reduce_factors(a, b, 1, store)
    d = si[0] + jnp.where(kx == 0, 1.0, 2.0)
    r = jnp.full((ny, nz), jnp.where(kx == 0, 0.0, 1.0), F32)
    phx[0] = r
    for x in range(nx):
        e = 1.0 / d
        ex[x] = e
        if x < nx - 1:
            d = si[x + 1] + (2.0 - e)
            r = e * r
            phx[x + 1] = r
    u = ex[nx - 1] * r
    w = ex[nx - 1] * jnp.where(kx == nxd - 1, 0.0, 1.0)
    phx[nx - 1] = u
    psx[nx - 1] = w
    cx[2] = w
    for x in range(nx - 2, -1, -1):
        u = ex[x] * (phx[x] + u)
        w = ex[x] * w
        phx[x] = u
        psx[x] = w
    cx[0] = u
    cx[1] = w


def z_load(zk, x):
    return lambda level: (zk[2 * level, x], zk[2 * level + 1, x])


def chain_x_kernel(el, mg, ds, si, e1_up, iz_out, up_out, pair):
    ky = lax.axis_index("gy")
    nx, ny, nz = ds.shape
    for x in range(nx):
        above = el[1, x + 1] if x < nx - 1 else e1_up[0]
        iz = mg[2, x] - H * (above - el[1, x])
        iz_out[x] = iz
        h1 = mg[1, x]
        rhs = ds[x] * el[0, x] + ((iz - prev_y(iz, 0.0)) - (h1 - prev_z(h1))) * (1.0 / H)
        kept, inv = y_factors(si[x], ky)
        u = reduce_apply(rhs, 0, kept.__getitem__, inv)
        up_out[x] = u
        pair[0, x:x + 1] = u[0:1]
        pair[1, x:x + 1] = u[ny - 1:ny] - iz[ny - 1:ny] * (1.0 / H)


def chain_z_kernel(el, mg, ds, ex, halo_y, iy_out, up_out, pair):
    nx, ny, nz = ds.shape
    rhs = []
    below = jnp.zeros((ny, nz), F32)
    for x in range(nx):
        e0 = el[0, x]
        iy = mg[1, x] - H * (next_z(e0) - e0)
        iy_out[x] = iy
        h0 = mg[0, x]
        rhs.append(ds[x] * el[2, x] + ((iy - below) - (h0 - prev_y(h0, halo_y[0, x:x + 1]))) * (1.0 / H))
        below = iy
    sweep_x(rhs, ex, up_out)
    pair[0] = up_out[0]
    pair[1] = up_out[nx - 1] - below * (1.0 / H)


def center_y_kernel(el, mg, ds, zk, zib, halo_y, h2_low, sx_out, t1_out):
    nx, ny, nz = ds.shape
    for x in range(nx):
        e2 = el[2, x]
        ix = mg[0, x] - H * (next_y(e2, halo_y[1, x:x + 1]) - e2)
        below = mg[2, x - 1] if x > 0 else h2_low[0]
        rhs = ds[x] * el[1, x] + ((ix - prev_z(ix)) - (mg[2, x] - below)) * (1.0 / H)
        cy = reduce_apply(rhs, 1, z_load(zk, x), zib[x])
        curl = H * (next_z(cy) - cy)
        mx = ix + curl
        sx_out[x] = mx + curl
        t1_out[x] = ds[x] * cy + (mx - prev_z(mx)) * (1.0 / H)


def scan_y_kernel(ready, recv, own, pair, weights, consts, send, halo, mixed):
    ky = lax.axis_index("gy")
    n = recv.shape[0]
    halo[0] = jnp.where(ky == 0, 0.0, recv[jnp.maximum(ky - 1, 0), 3])
    halo[1] = jnp.where(ky == n - 1, 0.0, recv[jnp.minimum(ky + 1, n - 1), 3])
    interface_factors(lambda j: (recv[j, 0], recv[j, 1], recv[j, 2]), (own[0], own[1], own[2]),
                      n, ky, weights, mixed, consts)
    ready()
    fill_send(send, pair[0], pair[1], consts, n, ky)


def half_x_kernel(nxd, ready, recv, weights, consts, up, iz, t1, ds, phy, psy, ex, coef_x, pair_z, sz_out, t4_out, ufy_out, send, edge):
    ky = lax.axis_index("gy")
    nx, ny, nz = ds.shape
    A, C = gather_sums(recv, weights, recv.shape[0], ky)
    for x in range(nx):
        edge[0, x:x + 1] = up[x][0:1]
        edge[1, x:x + 1] = up[x][ny - 1:ny] - iz[x][ny - 1:ny] * (1.0 / H)
    lower, upper = boundary(A, C, edge[0], edge[1], consts)
    edge[0] = lower
    edge[1] = upper
    ready()
    rhs = []
    below = jnp.zeros((ny, nz), F32)
    for x in range(nx):
        lo = edge[0, x:x + 1]
        hi = edge[1, x:x + 1]
        cx = up[x] + phy[x] * lo + psy[x] * hi
        curl = H * (next_y(cx, hi) - cx)
        mz = iz[x] + curl
        sz = mz + curl
        sz_out[x] = sz
        mlow = jnp.where(ky == 0, 0.0, H * (cx[0:1] - lo))
        t4_out[x] = ds[x] * cx + (mz - prev_y(mz, mlow)) * (1.0 / H)
        rhs.append(t1[x] - (sz - below) * (1.0 / H))
        below = sz
    sweep_x(rhs, ex, ufy_out)
    f = ufy_out[0]
    l = ufy_out[nx - 1] + below * (1.0 / H)
    for j in range(nxd):
        for i in range(3):
            send[j, i] = coef_x[i]
        send[j, 3] = pair_z[0]
        send[j, 4] = pair_z[1]
        send[j, 5] = f
        send[j, 6] = l


def half_z_kernel(ready, recv, cx, pair_z, up, iy, sx, ufy, sz, ds, phx, psx, si, consts_y, sy_out, ufz_out, pair_out, edge_y_out, send, weights, mixed, consts):
    kx = lax.axis_index("gx")
    ky = lax.axis_index("gy")
    nx, ny, nz = ds.shape
    n = recv.shape[0]
    interface_factors(lambda j: (recv[j, 0], recv[j, 1], recv[j, 2]), (cx[0], cx[1], cx[2]), n, kx, weights, mixed, consts)
    A, C = gather_sums_pair(lambda j: (recv[j, 5], recv[j, 6]), weights, mixed, n, kx)
    ready()
    lower, upper = boundary(A, C, ufy[0], ufy[nx - 1] + sz[nx - 1] * (1.0 / H), consts)
    edge_y_out[0] = lower
    edge_y_out[1] = upper
    A, C = gather_sums_pair(lambda j: (recv[j, 3], recv[j, 4]), weights, mixed, n, kx)
    lower, upper = boundary(A, C, pair_z[0], pair_z[1], consts)
    cz = up[0] + phx[0] * lower + psx[0] * upper
    below = jnp.where(kx == 0, 0.0, H * (cz - lower))
    for x in range(nx):
        cn = up[x + 1] + phx[x + 1] * lower + psx[x + 1] * upper if x < nx - 1 else upper
        curl = H * (cn - cz)
        my = iy[x] + curl
        sy_out[x] = my + curl
        s = sx[x]
        rhs = ds[x] * cz + ((my - below) - (s - prev_y(s, 0.0))) * (1.0 / H)
        kept, inv = y_factors(si[x], ky)
        u = reduce_apply(rhs, 0, kept.__getitem__, inv)
        ufz_out[x] = u
        pair_out[0, x:x + 1] = u[0:1]
        pair_out[1, x:x + 1] = u[ny - 1:ny] + s[ny - 1:ny] * (1.0 / H)
        cz = cn
        below = my
    fill_send(send, pair_out[0], pair_out[1], consts_y, send.shape[0], ky)


def final_x_kernel(t4, sy, si, fx_out, my_out):
    nx = t4.shape[0]
    for x in range(nx):
        s = sy[x]
        fx = z_solve(si[x], t4[x] - (s - prev_z(s)) * (1.0 / H))
        fx_out[x] = fx
        my_out[x] = s - H * (next_z(fx) - fx)


def final_y_kernel(edge, up, sz, phx, psx, fy_out, mz_out):
    nx = up.shape[0]
    lower = edge[0]
    upper = edge[1]
    fy = up[0] + phx[0] * lower + psx[0] * upper
    for x in range(nx):
        fn = up[x + 1] + phx[x + 1] * lower + psx[x + 1] * upper if x < nx - 1 else upper
        fy_out[x] = fy
        mz_out[x] = sz[x] - H * (fn - fy)
        fy = fn


def final_z_kernel(ready, recv, weights, consts, pair, up, sx, phy, psy, fx, fy, my, mz, e_out, h_out, edge):
    ky = lax.axis_index("gy")
    nx = up.shape[0]
    A, C = gather_sums(recv, weights, recv.shape[0], ky)
    lower, upper = boundary(A, C, pair[0], pair[1], consts)
    ready()
    edge[0] = lower
    edge[1] = upper
    for x in range(nx):
        lo = edge[0, x:x + 1]
        hi = edge[1, x:x + 1]
        fz = up[x] + phy[x] * lo + psy[x] * hi
        e_out[0, x] = fx[x]
        e_out[1, x] = fy[x]
        e_out[2, x] = fz
        h_out[0, x] = sx[x] - H * (next_y(fz, hi) - fz)
        h_out[1, x] = my[x]
        h_out[2, x] = mz[x]


def staged(kernel, kinds_in, kinds_out, first, late):
    def body(*refs):
        ni = len(kinds_in)
        no = len(kinds_out)
        ins = refs[:ni]
        outs = refs[ni:ni + no]
        rest = list(refs[ni + no:])
        sems = rest.pop()
        work = []
        copies = []
        for ref, kind in zip(ins, kinds_in):
            if kind == "v":
                work.append(ref)
                continue
            held = rest.pop(0)
            copy = pltpu.make_async_copy(ref, held, sems.at[len(copies)])
            if not late or len(copies) < first:
                copy.start()
            copies.append(copy)
            work.append(held)
        back = []
        for ref, kind in zip(outs, kinds_out):
            if kind == "v":
                work.append(ref)
                continue
            held = rest.pop(0)
            back.append((held, ref))
            work.append(held)
        head = len(copies) if first is None else first
        for copy in copies[:head]:
            copy.wait()

        if late:
            for copy in copies[head:]:
                copy.start()

        def ready():
            for copy in copies[head:]:
                copy.wait()

        if first is None:
            kernel(*work, *rest)
        else:
            kernel(ready, *work, *rest)
        copies = [pltpu.make_async_copy(held, ref, sems.at[i]) for i, (held, ref) in enumerate(back)]
        for copy in copies:
            copy.start()
        for copy in copies:
            copy.wait()

    return body


def call(kernel, outs, *args, smem=(), near=(), near_out=(), scratch=(), first=None, room=ROOM, hot=False, far=(), name=None):
    kinds_in = ["s" if i in smem else "v" if i in near or (hot and i not in far) else "h" for i in range(len(args))]
    kinds_out = ["v" if i in near_out or (hot and name.startswith(("final_x", "final_y"))) else "h" for i in range(len(outs))]
    held = []
    for a, kind in zip(args, kinds_in):
        if kind != "v":
            held.append((pltpu.SMEM if kind == "s" else pltpu.VMEM)(a.shape, a.dtype))
    for o, kind in zip(outs, kinds_out):
        if kind != "v":
            held.append(pltpu.VMEM(o, F32))
    spec = {"v": pltpu.VMEM, "h": HBM, "s": HBM}
    nbytes = sum(4 * _size(a.shape) for a in args) + sum(4 * _size(o) for o in outs)
    return pl.pallas_call(
        staged(kernel, kinds_in, kinds_out, 0 if hot and first is not None else first, name == "coef"),
        out_shape=[jax.ShapeDtypeStruct(o, F32) for o in outs],
        in_specs=[pl.BlockSpec(memory_space=spec[k]) for k in kinds_in],
        out_specs=[pl.BlockSpec(memory_space=spec[k]) for k in kinds_out],
        scratch_shapes=held + list(scratch) + [pltpu.SemaphoreType.DMA((max(len(held), 1),))],
        cost_estimate=pl.CostEstimate(flops=4 * nbytes, bytes_accessed=nbytes, transcendentals=0),
        compiler_params=pltpu.CompilerParams(vmem_limit_bytes=room << 20),
        name=name,
    )(*args)


def _size(shape):
    n = 1
    for d in shape:
        n *= d
    return n


def shifted(array, axis, by):
    count = lax.axis_size(axis)
    return lax.ppermute(array, axis, [(i, i + by) for i in range(count) if 0 <= i + by < count])


def exchange(array, axis):
    return lax.all_to_all(array, axis, 0, 0)


def per_device(electric, magnetic, material, permittivity, conductivity):
    nxd = lax.axis_size("gx")
    nyd = lax.axis_size("gy")
    cell = material.shape
    nx, ny, nz = cell
    py = (nx, nz)
    px = (ny, nz)

    def bind(kernel, *lead):
        def body(*refs):
            kernel(*lead, *refs)
        return body


    ds, si, phy, psy, cy, send_c, pe1, ph2 = call(
        bind(coef_kernel, nyd),
        [cell, cell, cell, cell, (3,) + py, (nyd, 4) + py,
         (1,) + px, (1,) + px],
        material, permittivity, conductivity, electric, magnetic, smem=(1, 2), first=3, room=60,
        scratch=[pltpu.VMEM(py, F32), pltpu.VMEM(py, F32)], name="coef")
    recv_c = exchange(send_c, "gy")
    e1_up = shifted(pe1, "gx", -1)
    h2_low = shifted(ph2, "gx", 1)
    zk, zib, ex, phx, psx, cx = call(
        bind(factor_kernel, nxd), [(2 * len(strides(nz)),) + cell, cell, cell, cell, cell, (3,) + px], si, name="factor")
    e1_up, h2_low, cx = lax.optimization_barrier((e1_up, h2_low, cx))
    iz, ux, pair_x = call(chain_x_kernel, [cell, cell, (2,) + py],
                          electric, magnetic, ds, si, e1_up, hot=True, far=(0, 1), room=40, name="chain_x")
    wy, ky, send1, halo_y = call(scan_y_kernel, [(nyd,) + py, (9,) + py, (nyd,) + py, (2,) + py], recv_c, cy, pair_x,
                         first=2, scratch=[pltpu.VMEM((nyd,) + py, F32)], hot=True, room=40, name="scan_y")
    recv1 = exchange(send1, "gy")

    iy, uz, pair_z = call(chain_z_kernel, [cell, cell, (2,) + px], electric, magnetic, ds, ex, halo_y, name="chain_z")
    sx, t1 = call(center_y_kernel, [cell, cell], electric, magnetic, ds, zk, zib, halo_y, h2_low, name="center_y")

    sz, t4, ufy, send2 = call(
        bind(half_x_kernel, nxd), [cell, cell, cell, (nxd, 7) + px],
        recv1, wy, ky, ux, iz, t1, ds, phy, psy, ex, cx, pair_z,
        first=4, scratch=[pltpu.VMEM((2,) + py, F32)], hot=True, room=40, name="half_x")
    recv2 = exchange(send2, "gx")
    sy, ufz, pair4, edge_y, send3 = call(
        half_z_kernel, [cell, cell, (2,) + py, (2,) + px, (nyd,) + py],
        recv2, cx, pair_z, uz, iy, sx, ufy, sz, ds, phx, psx, si, ky,
        first=2, scratch=[pltpu.VMEM((nxd,) + px, F32), pltpu.VMEM((nxd,) + px, F32), pltpu.VMEM((9,) + px, F32)],
        hot=True, room=40, name="half_z")
    recv3 = exchange(send3, "gy")
    fx, my = call(final_x_kernel, [cell, cell], t4, sy, si, hot=True, room=40, name="final_x")
    fy, mz = call(final_y_kernel, [cell, cell], edge_y, ufy, sz, phx, psx, hot=True, room=40, name="final_y")
    e, h = call(final_z_kernel, [(3,) + cell, (3,) + cell],
                recv3, wy, ky, pair4, ufz, sx, phy, psy, fx, fy, my, mz,
                first=4, scratch=[pltpu.VMEM((2,) + py, F32)], hot=True, room=40, name="final_z")
    return e, h


def solution(mesh):
    return jax.shard_map(
        per_device,
        mesh=mesh,
        in_specs=(
            P(None, "gx", "gy", None),
            P(None, "gx", "gy", None),
            P("gx", "gy", None),
            P(),
            P(),
        ),
        out_specs=(P(None, "gx", "gy", None), P(None, "gx", "gy", None)),
        check_vma=False,
    )
```
